32 devices in a mesh: dp: 8 (over z, x), sect: 4 (over y, core).
Axes of the slice: x: 2, y: 2, z: 4, core: 2. Of those that a mesh axis runs over, the one named last changes fastest.
Arguments:
- queries: bfloat16 [8, 16, 8192], P('dp', None, 'sect'), may hold values from -5 to 5
- keys: bfloat16 [8, 16, 8192], P('dp', None, 'sect'), may hold values from -5 to 5
- values: bfloat16 [8, 16, 8192], P('dp', None, 'sect'), may hold values from -6 to 6
- residual: bfloat16 [8, 16, 8192], P('dp'), may hold values from -6 to 6
- labels: int32 [8, 16], P('dp'), may hold values from 0 to 2, as said below
- slot_modality: int32 [4], replicated, may hold values from 0 to 2, as said below
- gains: float32 [3, 8192], replicated, may hold values from 0.1 to 1.9
- up_weight: bfloat16 [4, 11008, 8192], P('sect', 'dp'), may hold values from -0.0625 to 0.0625
- down_weight: bfloat16 [4, 11008, 8192], P('sect', 'dp'), may hold values from -0.0546875 to 0.0546875
- cotangent: bfloat16 [8, 16, 8192], P('dp'), may hold values from -6 to 6
Outputs:
- output: bfloat16 [8, 16, 8192], P('dp', 'sect')
- residual_grad: bfloat16 [8, 16, 8192], P('dp', 'sect')
- query_grad: bfloat16 [8, 16, 8192], P('dp', None, 'sect')
- key_grad: bfloat16 [8, 16, 8192], P('dp', None, 'sect')
- value_grad: bfloat16 [8, 16, 8192], P('dp', None, 'sect')
- up_grad: bfloat16 [4, 11008, 8192], P('sect', 'dp')
- down_grad: bfloat16 [4, 11008, 8192], P('sect', 'dp')
- gain_grad: float32 [3, 8192], replicated
The draws below stay inside these ranges and needn't reach their ends.
Inputs may be any that keep to these rules, and one draw needn't show every extreme that they name: `labels`: every sequence holds exactly 8 text tokens (label 0); its other tokens are image or speech. `slot_modality`: text owns two slots, image one, speech one.
All inputs are finite; a program needn't handle non-finite values.
Results may differ from the reference program's by a relative error of at most 0.015.
The reference program's roundings to bfloat16 on the way count: a program that leaves them out, or rounds other values in their place, can miss the bound.
Values may be sent and summed in bfloat16 or wider, within the bound.
A program may use at most 192 MiB of HBM per device.

```python
import jax
import jax.numpy as jnp
from jax import lax

D = 8192
HD = 128
FH = 11008
MODALITIES = 3
L = 16
SEQS = 8
N_SECT = 4


def attention_pair(key):
    base_key = jax.random.fold_in(key, 7)
    first, second = jax.random.split(base_key, 2)
    shape = (SEQS, L, D)
    key_vals = jnp.clip(jax.random.normal(first, shape, jnp.float32), -5.0, 5.0)
    query_vals = jnp.clip(jax.random.normal(second, shape, jnp.float32), -5.0, 5.0)
    return (query_vals, key_vals)


def draw_queries(key, part):
    return attention_pair(key)[0].astype(jnp.bfloat16)


def draw_keys(key, part):
    return attention_pair(key)[1].astype(jnp.bfloat16)


def draw_labels(key, part):
    seq_keys = jax.random.split(jax.random.fold_in(key, 3), SEQS)
    orders = jax.vmap(lambda one_key: jax.random.permutation(one_key, L))(seq_keys)
    others = jax.random.randint(jax.random.fold_in(key, 5), (SEQS, L), 1, 3)
    return jnp.where(orders < L // 2, 0, others).astype(jnp.int32)


def draw_slot_modality(key, part):
    order = jax.random.permutation(jax.random.fold_in(key, 9), 4)
    table = jnp.array([0, 0, 1, 2], jnp.int32)
    return jnp.take(table, order).astype(jnp.int32)


def block_levels(own_key, shape, pieces, smallest, high):
    loudness, own = 1.0, jax.random.fold_in(own_key, 6)
    for dim, parts in pieces:
        draws = jnp.exp(jax.random.uniform(jax.random.fold_in(own, dim), (parts,), jnp.float32, smallest / len(pieces), high / len(pieces)))
        loudness = loudness * jnp.repeat(draws, shape[dim] // parts).reshape([-1 if axis == dim else 1 for axis in range(len(shape))])
    return loudness


def centred(key, dims, deviation, bound, pieces=(), dtype=jnp.bfloat16):
    values = deviation * jax.random.normal(key, dims, jnp.float32)
    if pieces:
        values = values * block_levels(key, dims, pieces, -0.22, 0.18)
    return jnp.clip(values, -bound, bound).astype(dtype)


def setup_inputs(seed: int = 0) -> dict:
    key_of = jax.random.split(jax.random.key(seed), 11)
    queries = draw_queries(jax.random.fold_in(key_of[10], 71), 0)
    keys = draw_keys(jax.random.fold_in(key_of[10], 71), 0)
    values = centred(key_of[2], (SEQS, L, D), 1.0, 6.0, ((0, 8), (2, 4)))
    residual = centred(key_of[3], (SEQS, L, D), 1.0, 6.0, ((0, 8),))
    labels = draw_labels(jax.random.fold_in(key_of[10], 71), 0)
    slot_modality = draw_slot_modality(jax.random.fold_in(key_of[10], 71), 0)
    gains = jnp.clip(1.0 + 0.18 * jax.random.normal(key_of[6], (MODALITIES, D), jnp.float32), 0.1, 1.9)
    up_weight = centred(key_of[7], (N_SECT, FH, D), D ** -0.5, 0.0625, ((0, 4), (1, 8)))
    down_weight = centred(key_of[8], (N_SECT, FH, D), FH ** -0.5, 0.0546875, ((0, 4), (1, 8)))
    cotangent = centred(key_of[9], (SEQS, L, D), 1.0, 6.0, ((0, 8),))
    return {"queries": queries, "keys": keys, "values": values, "residual": residual, "labels": labels, "slot_modality": slot_modality, "gains": gains, "up_weight": up_weight, "down_weight": down_weight, "cotangent": cotangent}


def causal_forward(queries, keys, values):
    seq_count, length, width = queries.shape
    head_count = width // HD
    query_f = queries.astype(jnp.float32).reshape(seq_count, length, head_count, HD)
    key_f = keys.astype(jnp.float32).reshape(seq_count, length, head_count, HD)
    value_f = values.astype(jnp.float32).reshape(seq_count, length, head_count, HD)
    scores = jnp.einsum('sqhd,skhd->shqk', query_f, key_f) * HD ** (-0.5)
    position = jnp.arange(length)
    causal = position[:, None] >= position[None, :]
    scores = jnp.where(causal, scores, -1e+30)
    probs = jax.nn.softmax(scores, axis=-1)
    probs_b = probs.astype(jnp.bfloat16)
    attended = jnp.einsum('shqk,skhd->sqhd', probs_b.astype(jnp.float32), value_f)
    return (attended.astype(jnp.bfloat16).reshape(seq_count, length, width), probs, probs_b)

def causal_backward(grad_out, queries, keys, values, attended, probs, probs_b):
    seq_count, length, width = queries.shape
    head_count = width // HD
    shape = (seq_count, length, head_count, HD)
    grad_f = grad_out.astype(jnp.float32).reshape(shape)
    query_f = queries.astype(jnp.float32).reshape(shape)
    key_f = keys.astype(jnp.float32).reshape(shape)
    value_f = values.astype(jnp.float32).reshape(shape)
    attended_f = attended.astype(jnp.float32).reshape(shape)
    value_grad = jnp.einsum('shqk,sqhd->skhd', probs_b.astype(jnp.float32), grad_f).astype(jnp.bfloat16)
    dprob = jnp.einsum('sqhd,skhd->shqk', grad_f, value_f)
    delta = jnp.einsum('sqhd,sqhd->shq', grad_f, attended_f)
    dscore = (probs * (dprob - delta[..., None]) * HD ** (-0.5)).astype(jnp.bfloat16).astype(jnp.float32)
    query_grad = jnp.einsum('shqk,skhd->sqhd', dscore, key_f).astype(jnp.bfloat16)
    key_grad = jnp.einsum('shqk,sqhd->skhd', dscore, query_f).astype(jnp.bfloat16)
    return (query_grad.reshape(seq_count, length, width), key_grad.reshape(seq_count, length, width), value_grad.reshape(seq_count, length, width))

def block_sum(left, weight):
    return jnp.dot(left, weight, preferred_element_type=jnp.float32)

def reference(queries, keys, values, residual, labels, slot_modality, gains, up_weight, down_weight, cotangent):
    attended, probs, probs_b = causal_forward(queries, keys, values)
    hidden = (residual.astype(jnp.float32) + attended.astype(jnp.float32)).astype(jnp.bfloat16)
    hidden_f = hidden.astype(jnp.float32).reshape(-1, D)
    token_labels = labels.reshape(-1)
    onehot = (token_labels[:, None] == jnp.arange(MODALITIES)[None, :]).astype(jnp.float32)
    gain_rows = gains[token_labels]
    inverse = lax.rsqrt(lax.optimization_barrier(jnp.mean(hidden_f * hidden_f, axis=-1, keepdims=True)) + 1e-05)
    normed_f = hidden_f * inverse
    normed = (normed_f * gain_rows).astype(jnp.bfloat16)
    grad_rows = cotangent.reshape(-1, D)
    ffn = jnp.zeros(hidden_f.shape, jnp.float32)
    norm_grad = jnp.zeros(hidden_f.shape, jnp.float32)
    up_grads = []
    down_grads = []
    for slot_number in range(N_SECT):
        keep_mask = (token_labels == slot_modality[slot_number])[:, None]
        slot_rows = jnp.where(keep_mask, normed, jnp.zeros((), jnp.bfloat16))
        slot_cot = jnp.where(keep_mask, grad_rows, jnp.zeros((), jnp.bfloat16))
        preact = jnp.dot(slot_rows, up_weight[slot_number].T, preferred_element_type=jnp.float32)
        activated = jax.nn.silu(preact).astype(jnp.bfloat16)
        ffn = ffn + block_sum(activated, down_weight[slot_number])
        back = jnp.dot(slot_cot, down_weight[slot_number].T, preferred_element_type=jnp.float32)
        sigma = jax.nn.sigmoid(preact)
        pre_grad = (back * sigma * (1.0 + preact * (1.0 - sigma))).astype(jnp.bfloat16)
        down_grads.append(jnp.dot(activated.T, slot_cot, preferred_element_type=jnp.float32).astype(jnp.bfloat16))
        up_grads.append(jnp.dot(pre_grad.T, slot_rows, preferred_element_type=jnp.float32).astype(jnp.bfloat16))
        norm_grad = norm_grad + block_sum(pre_grad, up_weight[slot_number])
    output = (hidden_f + ffn).astype(jnp.bfloat16).reshape(residual.shape)
    scaled = norm_grad * gain_rows
    hidden_grad = grad_rows.astype(jnp.float32) + inverse * (scaled - normed_f * lax.optimization_barrier(jnp.mean(scaled * normed_f, axis=-1, keepdims=True)))
    residual_grad = hidden_grad.astype(jnp.bfloat16).reshape(residual.shape)
    gain_grad = jnp.dot(onehot.T, norm_grad * normed_f, precision=lax.Precision.HIGHEST)
    query_grad, key_grad, value_grad = causal_backward(residual_grad, queries, keys, values, attended, probs, probs_b)
    return (output, residual_grad, query_grad, key_grad, value_grad, jnp.stack(up_grads), jnp.stack(down_grads), gain_grad)
```

```python
import functools

import jax
import jax.numpy as jnp
from jax import lax
from jax.experimental import pallas as pl
from jax.experimental.pallas import tpu as pltpu
from jax.sharding import PartitionSpec as P

HD = 128
MODALITIES = 3


def causal_forward(queries, keys, values):
    seq_count, length, width = queries.shape
    head_count = width // HD
    query_f = queries.astype(jnp.float32).reshape(seq_count, length, head_count, HD)
    key_f = keys.astype(jnp.float32).reshape(seq_count, length, head_count, HD)
    value_f = values.astype(jnp.float32).reshape(seq_count, length, head_count, HD)
    scores = jnp.einsum("sqhd,skhd->shqk", query_f, key_f) * HD ** (-0.5)
    position = jnp.arange(length)
    causal = position[:, None] >= position[None, :]
    scores = jnp.where(causal, scores, -1e30)
    probs = jax.nn.softmax(scores, axis=-1)
    probs_b = probs.astype(jnp.bfloat16)
    attended = jnp.einsum("shqk,skhd->sqhd", probs_b.astype(jnp.float32), value_f)
    return (attended.astype(jnp.bfloat16).reshape(seq_count, length, width), probs, probs_b)


def causal_backward(grad_out, queries, keys, values, attended, probs, probs_b):
    seq_count, length, width = queries.shape
    head_count = width // HD
    shape = (seq_count, length, head_count, HD)
    grad_f = grad_out.astype(jnp.float32).reshape(shape)
    query_f = queries.astype(jnp.float32).reshape(shape)
    key_f = keys.astype(jnp.float32).reshape(shape)
    value_f = values.astype(jnp.float32).reshape(shape)
    attended_f = attended.astype(jnp.float32).reshape(shape)
    value_grad = jnp.einsum("shqk,sqhd->skhd", probs_b.astype(jnp.float32), grad_f).astype(
        jnp.bfloat16
    )
    dprob = jnp.einsum("sqhd,skhd->shqk", grad_f, value_f)
    delta = jnp.einsum("sqhd,sqhd->shq", grad_f, attended_f)
    dscore = (
        (probs * (dprob - delta[..., None]) * HD ** (-0.5)).astype(jnp.bfloat16).astype(jnp.float32)
    )
    query_grad = jnp.einsum("shqk,skhd->sqhd", dscore, key_f).astype(jnp.bfloat16)
    key_grad = jnp.einsum("shqk,sqhd->skhd", dscore, query_f).astype(jnp.bfloat16)
    return (
        query_grad.reshape(seq_count, length, width),
        key_grad.reshape(seq_count, length, width),
        value_grad.reshape(seq_count, length, width),
    )


MESH = pl.DeviceIdType.MESH
VMEM_BYTES = 60 * 1024 * 1024


def remote(src, dst, send_sem, recv_sem, dp_index, sect_index):
    return pltpu.make_async_remote_copy(
        src_ref=src,
        dst_ref=dst,
        send_sem=send_sem,
        recv_sem=recv_sem,
        device_id=(dp_index, sect_index),
        device_id_type=MESH,
    )


def greet(peers):
    barrier = pltpu.get_barrier_semaphore()
    total = jnp.int32(0)
    for dp_index, sect_index, present in peers:
        if present is None:
            pl.semaphore_signal(barrier, inc=1, device_id=(dp_index, sect_index), device_id_type=MESH)
            total = total + 1
        else:

            @pl.when(present)
            def _():
                pl.semaphore_signal(
                    barrier, inc=1, device_id=(dp_index, sect_index), device_id_type=MESH
                )

            total = total + present.astype(jnp.int32)
    pl.semaphore_wait(barrier, total)


class LineGather:
    def __init__(self, buf, sems, lines, slot):
        self.buf, self.lines = buf, lines
        self.send_sems, self.recv_sems = sems
        self.slot = slot
        self.me = lax.axis_index("dp")
        self.sect = lax.axis_index("sect")
        self.outer, self.inner = self.me // 2, self.me % 2

    def copy(self, way, outer, target, incoming=False):
        inner = (1 - self.inner) if (incoming and way == 2) else self.inner
        block = self.buf.at[outer * 2 + inner]
        recv = 1 if way == 2 else 0
        return remote(
            block,
            block,
            self.send_sems.at[self.slot, way, outer],
            self.recv_sems.at[self.slot, recv, outer],
            target,
            self.sect,
        )

    def pass_up(self, outer):
        return self.copy(0, outer, jnp.minimum(self.outer + 1, self.lines - 1) * 2 + self.inner)

    def pass_down(self, outer):
        return self.copy(1, outer, jnp.maximum(self.outer - 1, 0) * 2 + self.inner)

    def pass_across(self, outer):
        return self.copy(2, outer, self.outer * 2 + 1 - self.inner)

    def start(self):
        outer = self.outer

        @pl.when(outer + 1 < self.lines)
        def _():
            self.pass_up(outer).start()

        @pl.when(outer > 0)
        def _():
            self.pass_down(outer).start()

        self.pass_across(outer).start()

    def relay(self, step):
        outer = self.outer

        @pl.when(outer - step >= 0)
        def _():
            block = outer - step
            self.pass_down(block).wait_recv()

            @pl.when(outer + 1 < self.lines)
            def _():
                self.pass_up(block).start()

            self.pass_across(block).start()

        @pl.when(outer + step < self.lines)
        def _():
            block = outer + step
            self.pass_up(block).wait_recv()

            @pl.when(outer > 0)
            def _():
                self.pass_down(block).start()

            self.pass_across(block).start()

    def finish(self):
        outer = self.outer
        for block in range(self.lines):
            self.copy(2, block, self.outer * 2 + 1 - self.inner, incoming=True).wait_recv()
            self.pass_across(block).wait_send()

            @pl.when((outer + 1 < self.lines) & (block <= outer))
            def _():
                self.pass_up(block).wait_send()

            @pl.when((outer > 0) & (block >= outer))
            def _():
                self.pass_down(block).wait_send()


def front_kernel(
    lines, slots, att_ref, res_ref, gain_ref, sel_ref, cot_ref, hidden_ref, norm_ref, rows_ref, cots_ref,
    att_all, send_sems, recv_sems, att_send, att_recv,
):
    me, sect = lax.axis_index("dp"), lax.axis_index("sect")
    outer, inner = me // 2, me % 2
    width = att_ref.shape[1]
    peers = [(me, lax.rem(sect + k, slots), None) for k in range(1, slots)]
    peers.append((outer * 2 + 1 - inner, sect, None))
    peers.append((jnp.minimum(outer + 1, lines - 1) * 2 + inner, sect, outer + 1 < lines))
    peers.append((jnp.maximum(outer - 1, 0) * 2 + inner, sect, outer > 0))
    sel = sel_ref[...]
    cots_ref[me] = jnp.dot(sel, cot_ref[...], preferred_element_type=jnp.float32).astype(jnp.bfloat16)
    greet(peers)
    copies = []
    for k in range(1, slots):
        target = lax.rem(sect + k, slots)
        copies.append(
            remote(att_ref, att_all.at[sect], att_send.at[k], att_recv.at[sect], me, target)
        )
        copies[-1].start()
    cots = LineGather(cots_ref, (send_sems, recv_sems), lines, 0)
    rows = LineGather(rows_ref, (send_sems, recv_sems), lines, 1)
    cots.start()
    att_all[sect] = att_ref[...]
    for k in range(1, slots):
        source = lax.rem(sect + k, slots)
        remote(att_ref, att_all.at[source], att_send.at[k], att_recv.at[source], me, source).wait_recv()
    square = jnp.zeros((res_ref.shape[0], 1), jnp.float32)
    for block in range(slots):
        cols = slice(block * width, (block + 1) * width)
        hid = (
            res_ref[:, cols].astype(jnp.float32) + att_all[block].astype(jnp.float32)
        ).astype(jnp.bfloat16)
        hidden_ref[:, cols] = hid
        hid_f = hid.astype(jnp.float32)
        square = square + jnp.sum(hid_f * hid_f, axis=-1, keepdims=True)
    inverse = lax.rsqrt(square / (slots * width) + 1e-05)
    norm_ref[...] = jnp.broadcast_to(inverse, norm_ref.shape)
    for block in range(slots):
        cols = slice(block * width, (block + 1) * width)
        normed = (hidden_ref[:, cols].astype(jnp.float32) * inverse * gain_ref[:, cols]).astype(
            jnp.bfloat16
        )
        rows_ref[me, :, cols] = jnp.dot(sel, normed, preferred_element_type=jnp.float32).astype(
            jnp.bfloat16
        )
    rows.start()
    for step in range(1, lines):
        cots.relay(step)
        rows.relay(step)
    cots.finish()
    rows.finish()
    for one in copies:
        one.wait_send()


def front(att, residual, gain_rows, selector, cotangent, dp, slots):
    length, width = residual.shape
    capacity = selector.shape[0]
    vm = pl.BlockSpec(memory_space=pltpu.VMEM)
    return pl.pallas_call(
        functools.partial(front_kernel, dp // 2, slots),
        out_shape=(
            jax.ShapeDtypeStruct((length, width), jnp.bfloat16),
            jax.ShapeDtypeStruct((length, 128), jnp.float32),
            jax.ShapeDtypeStruct((dp, capacity, width), jnp.bfloat16),
            jax.ShapeDtypeStruct((dp, capacity, width), jnp.bfloat16),
        ),
        in_specs=[vm] * 5,
        out_specs=(vm,) * 4,
        scratch_shapes=[
            pltpu.VMEM((slots,) + att.shape, jnp.bfloat16),
            pltpu.SemaphoreType.DMA((2, 3, dp // 2)),
            pltpu.SemaphoreType.DMA((2, 2, dp // 2)),
            pltpu.SemaphoreType.DMA((slots,)),
            pltpu.SemaphoreType.DMA((slots,)),
        ],
        compiler_params=pltpu.CompilerParams(
            collective_id=0, has_side_effects=True, vmem_limit_bytes=VMEM_BYTES
        ),
    )(att, residual, gain_rows, selector, cotangent)


def ffn_kernel(tail, rows_ref, cots_ref, up_ref, down_ref, out_ref, back_ref, upg_ref, downg_ref, out_acc, back_acc):
    step = pl.program_id(0)
    last = pl.num_programs(0) - 1
    full = up_ref.shape[0]

    @pl.when(step == 0)
    def _():
        out_acc[...] = jnp.zeros_like(out_acc)
        back_acc[...] = jnp.zeros_like(back_acc)

    def run(size):
        rows, cots = rows_ref[...], cots_ref[...]
        preact = contract_last(rows, up_ref[:size, :])
        back = contract_last(cots, down_ref[:size, :])
        sigma = jax.nn.sigmoid(preact)
        activated = (preact * sigma).astype(jnp.bfloat16)
        pre_grad = (back * sigma * (1.0 + preact * (1.0 - sigma))).astype(jnp.bfloat16)
        out_acc[...] += jnp.dot(activated, down_ref[:size, :], preferred_element_type=jnp.float32)
        back_acc[...] += jnp.dot(pre_grad, up_ref[:size, :], preferred_element_type=jnp.float32)
        downg_ref[:size, :] = contract_first(activated, cots).astype(jnp.bfloat16)
        upg_ref[:size, :] = contract_first(pre_grad, rows).astype(jnp.bfloat16)

    if tail == full:
        run(full)
    else:

        @pl.when(step < last)
        def _():
            run(full)

        @pl.when(step == last)
        def _():
            run(tail)

    @pl.when(step == last)
    def _():
        out_ref[...] = out_acc[...].astype(jnp.bfloat16)
        back_ref[...] = back_acc[...].astype(jnp.bfloat16)


def ffn(rows, cots, up, down):
    count, width = rows.shape
    hidden_units = up.shape[0]
    chunk = min(256 if count <= 128 else 128, hidden_units)
    steps = pl.cdiv(hidden_units, chunk)
    tail = hidden_units - (steps - 1) * chunk
    whole = pl.BlockSpec((count, width), lambda i: (0, 0))
    weight = pl.BlockSpec((chunk, width), lambda i: (i, 0))
    return pl.pallas_call(
        functools.partial(ffn_kernel, tail),
        grid=(steps,),
        out_shape=(
            jax.ShapeDtypeStruct((count, width), jnp.bfloat16),
            jax.ShapeDtypeStruct((count, width), jnp.bfloat16),
            jax.ShapeDtypeStruct(up.shape, jnp.bfloat16),
            jax.ShapeDtypeStruct(down.shape, jnp.bfloat16),
        ),
        in_specs=[whole, whole, weight, weight],
        out_specs=(whole, whole, weight, weight),
        scratch_shapes=[
            pltpu.VMEM((count, width), jnp.float32),
            pltpu.VMEM((count, width), jnp.float32),
        ],
        compiler_params=pltpu.CompilerParams(
            dimension_semantics=("arbitrary",), vmem_limit_bytes=VMEM_BYTES
        ),
    )(rows, cots, up, down)


def reduce_kernel(lines, slots, out_in, back_in, sums_ref, from_pair, pair_sum, from_line, pair_send, pair_recv,
                  line_send, line_recv, sect_send, sect_recv):
    me, sect = lax.axis_index("dp"), lax.axis_index("sect")
    outer, inner = me // 2, me % 2
    partner = outer * 2 + 1 - inner
    terms = (back_in, out_in)
    peers = [(me, lax.rem(sect + k, slots), None) for k in range(1, slots)]
    peers.append((partner, sect, None))
    for k in range(1, lines):
        peers.append((lax.rem(outer + k, lines) * 2 + inner, sect, None))
    greet(peers)
    order = [(k, step) for k in range(2) for step in list(range(1, lines)) + [0]]

    def across(k, step):
        line = lax.rem(outer + step, lines)
        return remote(
            terms[k].at[line * 2 + 1 - inner],
            from_pair.at[k, step],
            pair_send.at[k, step],
            pair_recv.at[k, step],
            partner,
            sect,
        )

    def along(k, step):
        line = lax.rem(outer + step, lines)
        return remote(
            pair_sum.at[k, step],
            from_line.at[k, step],
            line_send.at[k, step],
            line_recv.at[k, step],
            line * 2 + inner,
            sect,
        )

    def to_sect(k, hop):
        target = lax.rem(sect + hop, slots)
        return remote(
            sums_ref.at[k, sect],
            sums_ref.at[k, sect],
            sect_send.at[k, hop],
            sect_recv.at[k, sect],
            me,
            target,
        )

    def from_sect(k, hop):
        source = lax.rem(sect + hop, slots)
        return remote(
            sums_ref.at[k, source],
            sums_ref.at[k, source],
            sect_send.at[k, hop],
            sect_recv.at[k, source],
            me,
            source,
        )

    for k, step in order:
        across(k, step).start()
    for k in range(2):
        for step in list(range(1, lines)) + [0]:
            across(k, step).wait_recv()
            line = lax.rem(outer + step, lines)
            own = terms[k][line * 2 + inner].astype(jnp.float32) + from_pair[k, step].astype(jnp.float32)
            if step:
                pair_sum[k, step] = own.astype(jnp.bfloat16)
                along(k, step).start()
        for step in range(1, lines):
            along(k, step).wait_recv()
            own = own + from_line[k, step].astype(jnp.float32)
        sums_ref[k, sect] = own.astype(jnp.bfloat16)
        for hop in range(1, slots):
            to_sect(k, hop).start()
    for k in range(2):
        for hop in range(1, slots):
            from_sect(k, hop).wait_recv()
            to_sect(k, hop).wait_send()
        for step in range(lines):
            across(k, step).wait_send()
            if step:
                along(k, step).wait_send()


def reduce_terms(out_terms, back_terms, slots):
    dp, capacity, width = out_terms.shape
    lines = dp // 2
    vm = pl.BlockSpec(memory_space=pltpu.VMEM)
    dma = pltpu.SemaphoreType.DMA
    return pl.pallas_call(
        functools.partial(reduce_kernel, lines, slots),
        out_shape=jax.ShapeDtypeStruct((2, slots, capacity, width), jnp.bfloat16),
        in_specs=[vm] * 2,
        out_specs=vm,
        scratch_shapes=[
            pltpu.VMEM((2, lines, capacity, width), jnp.bfloat16),
            pltpu.VMEM((2, lines, capacity, width), jnp.bfloat16),
            pltpu.VMEM((2, lines, capacity, width), jnp.bfloat16),
            dma((2, lines)),
            dma((2, lines)),
            dma((2, lines)),
            dma((2, lines)),
            dma((2, slots)),
            dma((2, slots)),
        ],
        compiler_params=pltpu.CompilerParams(
            collective_id=1, has_side_effects=True, vmem_limit_bytes=VMEM_BYTES
        ),
    )(out_terms, back_terms)


def gain_kernel(dp, slots, part_ref, total_ref, inbox, mine, first_send, first_recv, next_send, next_recv, sect_send, sect_recv):
    me, sect = lax.axis_index("dp"), lax.axis_index("sect")
    peers = [(me, lax.rem(sect + k, slots), None) for k in range(1, slots)]
    peers += [(lax.rem(me + k, dp), sect, None) for k in range(1, dp)]
    greet(peers)

    def scatter(k):
        target = lax.rem(me + k, dp)
        return remote(
            part_ref.at[sect, target], inbox.at[k], first_send.at[k], first_recv.at[k], target, sect
        )

    def spread_sum(k):
        target = lax.rem(me + k, dp)
        return remote(
            mine, total_ref.at[sect, me], next_send.at[k], next_recv.at[k], target, sect
        )

    def to_sect(k):
        return remote(
            total_ref.at[sect],
            total_ref.at[sect],
            sect_send.at[k],
            sect_recv.at[k],
            me,
            lax.rem(sect + k, slots),
        )

    for k in range(1, dp):
        scatter(k).start()
    total = part_ref[sect, me]
    for k in range(1, dp):
        scatter(k).wait_recv()
        total = total + inbox[k]
    mine[...] = total
    for k in range(1, dp):
        spread_sum(k).start()
    total_ref[sect, me] = total
    for k in range(1, dp):
        spread_sum(k).wait_recv()
    for k in range(1, slots):
        to_sect(k).start()
    for k in range(1, slots):
        to_sect(k).wait_recv()
        to_sect(k).wait_send()
    for k in range(1, dp):
        scatter(k).wait_send()
        spread_sum(k).wait_send()


def gain_sum(part, dp, slots):
    kinds, width = part.shape
    cols = width // (dp * slots)
    padded = jnp.concatenate([part, jnp.zeros((8 - kinds, width), part.dtype)], 0)
    pieces = padded.reshape(8, slots, dp, cols).transpose(1, 2, 0, 3)
    vm = pl.BlockSpec(memory_space=pltpu.VMEM)
    dma = pltpu.SemaphoreType.DMA
    total = pl.pallas_call(
        functools.partial(gain_kernel, dp, slots),
        out_shape=jax.ShapeDtypeStruct(pieces.shape, pieces.dtype),
        in_specs=[vm],
        out_specs=vm,
        scratch_shapes=[
            pltpu.VMEM((dp, 8, cols), pieces.dtype),
            pltpu.VMEM((8, cols), pieces.dtype),
            dma((dp,)),
            dma((dp,)),
            dma((dp,)),
            dma((dp,)),
            dma((slots,)),
            dma((slots,)),
        ],
        compiler_params=pltpu.CompilerParams(collective_id=2, has_side_effects=True),
    )(pieces)
    return total.transpose(2, 0, 1, 3).reshape(8, width)[:kinds]


def contract_last(left, right):
    return lax.dot_general(
        left, right, (((1,), (1,)), ((), ())), preferred_element_type=jnp.float32
    )


def contract_first(left, right):
    return lax.dot_general(
        left, right, (((0,), (0,)), ((), ())), preferred_element_type=jnp.float32
    )


def selectors(token_labels, slot_modality):
    length = token_labels.shape[0]
    keep = token_labels[None, :] == slot_modality[:, None]
    upto = jnp.arange(length)[None, :] <= jnp.arange(length)[:, None]
    rank = jnp.sum((keep[:, None, :] & upto[None]).astype(jnp.int32), axis=2) - 1
    capacity = length // 2
    return (rank[:, None, :] == jnp.arange(capacity)[None, :, None]) & keep[:, None, :]


def on_device(
    dp, slots, queries, keys, values, residual, labels, slot_modality, gains, up_weight, down_weight, cotangent
):
    attended_block, probs, probs_b = causal_forward(queries, keys, values)
    token_labels = labels[0]
    onehot = (token_labels[:, None] == jnp.arange(MODALITIES)[None, :]).astype(jnp.float32)
    gain_rows = jnp.dot(onehot, gains, precision=lax.Precision.HIGHEST)
    slot_index = lax.axis_index("sect")
    all_select = selectors(token_labels, slot_modality).astype(jnp.bfloat16)
    selector = lax.dynamic_index_in_dim(all_select, slot_index, 0, keepdims=False)
    capacity, length = selector.shape
    grad_full = cotangent[0]
    hidden, inverse, rows, cots = front(
        attended_block[0], residual[0], gain_rows, selector, grad_full, dp, slots
    )
    width = hidden.shape[1]
    inverse = inverse[:, :1]
    hidden_f = hidden.astype(jnp.float32)
    normed_f = hidden_f * inverse
    out_terms, back_terms, up_grad, down_grad = ffn(
        rows.reshape(-1, width), cots.reshape(-1, width), up_weight[0], down_weight[0]
    )
    sums = reduce_terms(
        out_terms.reshape(dp, capacity, width), back_terms.reshape(dp, capacity, width), slots
    ).reshape(2, slots * capacity, width)
    place = all_select.reshape(slots * capacity, length)
    norm_grad = contract_first(place, sums[0])
    quarter = length // slots
    place_own = lax.dynamic_slice_in_dim(place, slot_index * quarter, quarter, 1)
    hidden_own = lax.dynamic_slice_in_dim(hidden_f, slot_index * quarter, quarter, 0)
    output = (hidden_own + contract_first(place_own, sums[1])).astype(jnp.bfloat16)[None]
    scaled = norm_grad * gain_rows
    hidden_grad = grad_full.astype(jnp.float32) + inverse * (
        scaled - normed_f * jnp.mean(scaled * normed_f, axis=-1, keepdims=True)
    )
    residual_full = hidden_grad.astype(jnp.bfloat16)
    residual_grad = lax.dynamic_slice_in_dim(residual_full, slot_index * quarter, quarter, 0)[None]
    gain_part = jnp.dot(onehot.T, norm_grad * normed_f, precision=lax.Precision.HIGHEST)
    gain_grad = gain_sum(gain_part, dp, slots)
    block_width = queries.shape[2]
    grad_block = lax.dynamic_slice_in_dim(residual_full, slot_index * block_width, block_width, 1)[
        None
    ]
    query_grad, key_grad, value_grad = causal_backward(
        grad_block, queries, keys, values, attended_block, probs, probs_b
    )
    return (
        output, residual_grad, query_grad, key_grad, value_grad, up_grad[None], down_grad[None], gain_grad,
    )


def flip(index, offset):
    bit = 1
    while bit <= offset:
        if offset & bit:
            index = index + bit - 2 * bit * (lax.div(index, bit) % 2)
        bit *= 2
    return index


def block_mask(rows):
    row = lax.broadcasted_iota(jnp.int32, (rows, rows), 0)
    col = lax.broadcasted_iota(jnp.int32, (rows, rows), 1)
    return (row // LENGTH == col // LENGTH) & (col <= row)


def stack_heads(block):
    heads = block.shape[1] // HD
    return jnp.concatenate([block[:, h * HD : (h + 1) * HD] for h in range(heads)], axis=0)


def attend(query, key, value):
    scores = contract_last(query, key) * HD ** (-0.5)
    scores = jnp.where(block_mask(query.shape[0]), scores, -1e30)
    top = jnp.max(scores, axis=-1, keepdims=True)
    weight = jnp.exp(scores - top)
    probs = weight / jnp.sum(weight, axis=-1, keepdims=True)
    probs_b = probs.astype(jnp.bfloat16)
    attended = jnp.dot(probs_b, value, preferred_element_type=jnp.float32).astype(jnp.bfloat16)
    return attended, probs, probs_b


def layer_kernel(
    dims, labels_ref, modality_ref, query_hbm, key_hbm, value_hbm, residual_hbm, gains_hbm, up_hbm, down_hbm, cot_hbm,
    act_out, pre_grad_out, rows_out, sums_ref, gain_ref,
    up_w, down_w, rows_all, query_s, key_s, value_s, residual_s, gains_s, hidden_s, stat, tags, pre_t, back_t,
    act_t, pre_grad_t, act_n, pre_grad_n, parts, from_core, from_second, from_first, from_line, gain_mine, gain_inbox,
    gain_own, load_sem, weight_sem, tag_send, tag_recv, stat_send, stat_recv, line_send, line_recv, first_send, first_recv,
    second_send, second_recv, core_send, core_recv, r1_send, r1_recv, r2_send, r2_recv, r3_send, r3_recv,
    r4_send, r4_recv, spread_send, spread_recv, gs_send, gs_recv, gd_send, gd_recv, gx_send, gx_recv, store_sem,
):
    lines, dp, slots, quarter, hidden_units = dims
    width = quarter * slots
    d, s = lax.axis_index("dp"), lax.axis_index("sect")
    line, inner = lax.div(d, 2), d % 2
    y, c = lax.div(s, 2), s % 2
    tokens = dp * LENGTH

    core_id = (d, flip(s, 1))
    first_id = (d + (1 - c) * (1 - 2 * inner), s + c * 2 * (1 - 2 * y))
    second_id = (d + c * (1 - 2 * inner), s + (1 - c) * 2 * (1 - 2 * y))

    def send(src, dst, send_sem, recv_sem, target):
        return remote(src, dst, send_sem, recv_sem, target[0], target[1])

    def line_id(k):
        return (flip(line, k) * 2 + inner, s)

    def side(far_first, far_second):
        dy = far_second * (1 - c) + far_first * c
        di = far_first * (1 - c) + far_second * c
        return y + dy * (1 - 2 * y), inner + di * (1 - 2 * inner), dy * 2 + di

    mine = rows_all.at[0, s, inner, line]
    loads = [
        pltpu.make_async_copy(cot_hbm.at[0, :, pl.ds(pl.multiple_of(s * quarter, quarter), quarter)], mine, load_sem.at[0]),
        pltpu.make_async_copy(query_hbm.at[0], query_s, load_sem.at[1]),
        pltpu.make_async_copy(key_hbm.at[0], key_s, load_sem.at[2]),
        pltpu.make_async_copy(value_hbm.at[0], value_s, load_sem.at[3]),
        pltpu.make_async_copy(
            residual_hbm.at[0, :, pl.ds(pl.multiple_of(s * quarter, quarter), quarter)], residual_s, load_sem.at[4]
        ),
        pltpu.make_async_copy(gains_hbm, gains_s, load_sem.at[5]),
    ]
    for one in loads:
        one.start()
    order = [y * 2, y * 2 + 1, (1 - y) * 2, (1 - y) * 2 + 1]

    def weight_load(which, step):
        src, dst = ((down_hbm, down_w), (up_hbm, up_w))[which]
        at = order[step]
        return pltpu.make_async_copy(
            src.at[0, :, pl.ds(pl.multiple_of(at * quarter, quarter), quarter)], dst.at[at], weight_sem.at[which, step]
        )

    for which in range(2):
        for step in range(slots):
            weight_load(which, step).start()

    lane = lax.broadcasted_iota(jnp.int32, (8, tokens), 1)
    sub = lax.broadcasted_iota(jnp.int32, (LENGTH, HD), 0)
    base = (inner * lines + line) * LENGTH
    tag = jnp.zeros((8, tokens), jnp.float32)
    own_tag = jnp.zeros((LENGTH, HD), jnp.float32)
    for t in range(LENGTH):
        value = labels_ref[0, t].astype(jnp.float32)
        tag = jnp.where(lane == base + t, value, tag)
        own_tag = jnp.where(sub == t, value, own_tag)
    tags[0] = tag

    barrier = pltpu.get_barrier_semaphore()
    for k in range(1, dp):
        pl.semaphore_signal(barrier, inc=1, device_id=(flip(d, k), s), device_id_type=MESH)
    for k in range(1, slots):
        pl.semaphore_signal(barrier, inc=1, device_id=(d, flip(s, k)), device_id_type=MESH)
    pl.semaphore_wait(barrier, dp - 1 + slots - 1)

    def on_line(a, k, where):
        block = rows_all.at[a, s, inner, where]
        return send(block, block, line_send.at[a, k], line_recv.at[a, k], line_id(k))

    def on_first(a, k):
        block = rows_all.at[a, s, inner, flip(line, k)]
        return send(block, block, first_send.at[a, k], first_recv.at[a, k], first_id)

    def on_second(a, f, k):
        gy, gi, _ = side(f, 0)
        block = rows_all.at[a, gy * 2 + c, gi, flip(line, k)]
        return send(block, block, second_send.at[a, f, k], second_recv.at[a, f, k], second_id)

    def on_core(a, f, g):
        gy, gi, place = side(f, g)
        group = rows_all.at[a, gy * 2 + c, gi]
        return send(group, group, core_send.at[a, place], core_recv.at[a, place], core_id)

    def gather_start(a):
        for k in range(1, lines):
            on_line(a, k, line).start()
        on_first(a, 0).start()
        on_second(a, 0, 0).start()

    def gather_line(a):
        for k in range(1, lines):
            on_line(a, k, line).wait_recv()
            on_first(a, k).start()
            on_second(a, 0, k).start()
        on_core(a, 0, 0).start()

    def gather_first(a):
        for k in range(lines):
            on_first(a, k).wait_recv()
            on_second(a, 1, k).start()
        on_core(a, 1, 0).start()

    def gather_second(a):
        for f in range(2):
            for k in range(lines):
                on_second(a, f, k).wait_recv()
            on_core(a, f, 1).start()

    def gather_core(a, dy):
        for di in range(2):
            group = rows_all.at[a, 0, 0]
            send(group, group, core_send.at[a, dy * 2 + di], core_recv.at[a, dy * 2 + di], core_id).wait_recv()

    def gather_end(a):
        for k in range(1, lines):
            on_line(a, k, line).wait_send()
        for k in range(lines):
            on_first(a, k).wait_send()
            for f in range(2):
                on_second(a, f, k).wait_send()
        for f in range(2):
            for g in range(2):
                on_core(a, f, g).wait_send()

    def send_tag(k):
        return send(tags.at[0], tags.at[k], tag_send.at[k], tag_recv.at[k], (flip(d, k), s))

    def send_stat(turn, k):
        return send(stat.at[turn, 0], stat.at[turn, k], stat_send.at[turn, k], stat_recv.at[turn, k], (d, flip(s, k)))

    loads[0].wait()
    gather_start(0)
    for k in range(1, dp):
        send_tag(k).start()
    for one in loads[1:]:
        one.wait()

    attended, _, _ = attend(stack_heads(query_s[...]), stack_heads(key_s[...]), stack_heads(value_s[...]))
    square = jnp.zeros((LENGTH, 1), jnp.float32)
    for h in range(quarter // HD):
        cols = slice(h * HD, (h + 1) * HD)
        hid = (
            residual_s[:, cols].astype(jnp.float32) + attended[h * LENGTH : (h + 1) * LENGTH, :].astype(jnp.float32)
        ).astype(jnp.bfloat16)
        hidden_s[:, cols] = hid
        hid_f = hid.astype(jnp.float32)
        square = square + jnp.sum(hid_f * hid_f, axis=-1, keepdims=True)
    stat[0, 0] = jnp.broadcast_to(square, (LENGTH, HD))
    for k in range(1, slots):
        send_stat(0, k).start()
    gather_line(0)
    for k in range(1, slots):
        send_stat(0, k).wait_recv()
    total = (stat[0, 0] + stat[0, 1] + stat[0, 2] + stat[0, 3])[:, :1]
    inverse = lax.rsqrt(total / width + 1e-05)

    def gain_rows():
        g = gains_s[:, pl.ds(pl.multiple_of(s * quarter, quarter), quarter)]
        own = own_tag[:, :1]
        return jnp.where(own == 0.0, g[0:1, :], jnp.where(own == 1.0, g[1:2, :], g[2:3, :]))

    rows_all[1, s, inner, line] = (hidden_s[...].astype(jnp.float32) * inverse * gain_rows()).astype(jnp.bfloat16)
    gather_start(1)
    gather_first(0)
    gather_line(1)
    gather_second(0)

    half = hidden_units // 2

    def project(a, step):
        dst, weight = ((back_t, down_w), (pre_t, up_w))[a]
        weight_load(a, step).wait()
        at = order[step]
        block = rows_all[a, at].reshape(tokens, quarter)
        for h in (0, half):
            term = contract_last(weight[at, h : h + half, :], block)
            if step == 0:
                dst[h : h + half, :] = term
            else:
                dst[h : h + half, :] += term

    gather_core(0, 0)
    project(0, 0)
    gather_first(1)
    project(0, 1)
    gather_core(0, 1)
    project(0, 2)
    gather_second(1)
    project(0, 3)
    gather_core(1, 0)
    project(1, 0)
    project(1, 1)
    gather_core(1, 1)
    project(1, 2)
    project(1, 3)
    keep_rows = pltpu.make_async_copy(rows_all, rows_out, store_sem.at[0])
    keep_rows.start()

    for k in range(1, dp):
        send_tag(k).wait_recv()
    all_tags = tags[0]
    for k in range(1, dp):
        all_tags = all_tags + tags[k]
    modality = modality_ref[s].astype(jnp.float32)
    keep = all_tags[:1, :] == modality
    preact = pre_t[...]
    sigma = jax.nn.sigmoid(preact)
    activated = jnp.where(keep, preact * sigma, 0.0)
    pre_grad = jnp.where(keep, back_t[...] * sigma * (1.0 + preact * (1.0 - sigma)), 0.0)
    act_t[...] = activated.astype(jnp.bfloat16)
    pre_grad_t[...] = pre_grad.astype(jnp.bfloat16)
    pre_grad_n[...] = pre_grad.T.astype(jnp.bfloat16)
    act_n[...] = activated.T.astype(jnp.bfloat16)
    keep_act = pltpu.make_async_copy(act_t, act_out, store_sem.at[1])
    keep_pre_grad = pltpu.make_async_copy(pre_grad_t, pre_grad_out, store_sem.at[2])
    keep_act.start()
    keep_pre_grad.start()

    def to_core(a, dy):
        gy = y + dy * (1 - 2 * y)
        return send(parts.at[a, gy * 2 + 1 - c], from_core.at[a, dy], r1_send.at[a, dy], r1_recv.at[a, dy], core_id)

    def to_second(a, f):
        gy, gi, _ = side(f, 1)
        return send(parts.at[a, gy * 2 + c, gi], from_second.at[a, f], r2_send.at[a, f], r2_recv.at[a, f], second_id)

    def to_first(a):
        gy, gi, _ = side(1, 0)
        return send(parts.at[a, gy * 2 + c, gi], from_first.at[a], r3_send.at[a], r3_recv.at[a], first_id)

    def to_line(a, k):
        block = parts.at[a, s, inner, flip(line, k)]
        return send(block, from_line.at[a, k], r4_send.at[a, k], r4_recv.at[a, k], line_id(k))

    def partial_sum(a, at):
        source, weight = ((pre_grad_n, up_w), (act_n, down_w))[a]
        term = jnp.dot(source[...], weight[at], preferred_element_type=jnp.float32)
        parts[a, at] = term.astype(jnp.bfloat16).reshape(parts.shape[2:])
        if a == 0:
            rows = rows_all[1, at].reshape(tokens, quarter).astype(jnp.float32)
            g = gains_s[:, pl.ds(pl.multiple_of(at * quarter, quarter), quarter)]
            own = jnp.where(modality == 0.0, g[0:1, :], jnp.where(modality == 1.0, g[1:2, :], g[2:3, :]))
            total = jnp.sum(term * rows, axis=0, keepdims=True) / own
            chunk = width // dp
            for j in range(quarter // chunk):
                for r in range(8):
                    first = j * chunk + r * HD
                    gain_mine[at * (quarter // chunk) + j, r : r + 1, :] = total[:, first : first + HD]

    def add(dst, src):
        dst[...] = (dst[...].astype(jnp.float32) + src[...].astype(jnp.float32)).astype(jnp.bfloat16)

    def core_sums(a):
        other = (1 - y) * 2
        partial_sum(a, other + 1 - c)
        to_core(a, 1).start()
        partial_sum(a, other + c)
        partial_sum(a, y * 2 + 1 - c)
        to_core(a, 0).start()
        to_core(a, 1).wait_recv()
        add(parts.at[a, other + c], from_core.at[a, 1])
        to_second(a, 1).start()
        partial_sum(a, s)
        to_core(a, 0).wait_recv()
        add(parts.at[a, s], from_core.at[a, 0])
        to_second(a, 0).start()

    def second_sums(a):
        for f in (1, 0):
            to_second(a, f).wait_recv()
            gy, gi, _ = side(f, 0)
            add(parts.at[a, gy * 2 + c, gi], from_second.at[a, f])
            if f:
                to_first(a).start()

    def first_sums(a):
        to_first(a).wait_recv()
        add(parts.at[a, s, inner], from_first.at[a])
        for k in range(1, lines):
            to_line(a, k).start()

    def line_sums(a):
        total = parts[a, s, inner, line].astype(jnp.float32)
        for k in range(1, lines):
            to_line(a, k).wait_recv()
            total = total + from_line[a, k].astype(jnp.float32)
        return total

    def gain_scatter(k):
        target = flip(d, k)
        return send(gain_mine.at[target], gain_inbox.at[k], gs_send.at[k], gs_recv.at[k], (target, s))

    def gain_spread(k):
        return send(gain_own, gain_ref.at[s, d], gd_send.at[k], gd_recv.at[k], (flip(d, k), s))

    def gain_across(k):
        return send(gain_ref.at[s], gain_ref.at[s], gx_send.at[k], gx_recv.at[k], (d, flip(s, k)))

    def spread(a, k):
        return send(sums_ref.at[a, s], sums_ref.at[a, s], spread_send.at[a, k], spread_recv.at[a, k], (d, flip(s, k)))

    core_sums(0)
    for k in range(1, dp):
        gain_scatter(k).start()
    core_sums(1)
    second_sums(0)
    gain_total = gain_mine[d]
    for k in range(1, dp):
        gain_scatter(k).wait_recv()
        gain_total = gain_total + gain_inbox[k]
    gain_own[...] = gain_total
    gain_ref[s, d] = gain_total
    for k in range(1, dp):
        gain_spread(k).start()
    first_sums(0)
    second_sums(1)
    norm_grad = line_sums(0)
    hid_f = hidden_s[...].astype(jnp.float32)
    normed_f = hid_f * inverse
    scaled = norm_grad * gain_rows()
    own_stat = jnp.sum(scaled * normed_f, axis=-1, keepdims=True)
    stat[1, 0] = jnp.broadcast_to(own_stat, (LENGTH, HD))
    for k in range(1, slots):
        send_stat(1, k).start()
    first_sums(1)
    for k in range(1, dp):
        gain_spread(k).wait_recv()
    for k in range(1, slots):
        gain_across(k).start()
    for k in range(1, slots):
        send_stat(1, k).wait_recv()
    mean = (stat[1, 0] + stat[1, 1] + stat[1, 2] + stat[1, 3])[:, :1] / width
    cot_f = rows_all[0, s, inner, line].astype(jnp.float32)
    sums_ref[0, s] = (cot_f + inverse * (scaled - normed_f * mean)).astype(jnp.bfloat16)
    for k in range(1, slots):
        spread(0, k).start()
    sums_ref[1, s] = (hidden_s[...].astype(jnp.float32) + line_sums(1)).astype(jnp.bfloat16)
    for k in range(1, slots):
        spread(1, k).start()
    keep_rows.wait()
    keep_act.wait()
    keep_pre_grad.wait()
    for a in range(2):
        gather_end(a)
        for k in range(1, slots):
            send_stat(a, k).wait_send()
        for f in range(2):
            to_core(a, f).wait_send()
            to_second(a, f).wait_send()
        to_first(a).wait_send()
        for k in range(1, lines):
            to_line(a, k).wait_send()
    for k in range(1, dp):
        send_tag(k).wait_send()
        gain_scatter(k).wait_send()
        gain_spread(k).wait_send()
    for k in range(1, slots):
        gain_across(k).wait_recv()
        gain_across(k).wait_send()
    for a in range(2):
        for k in range(1, slots):
            spread(a, k).wait_recv()
            spread(a, k).wait_send()


LENGTH = 16


def layer(dp, slots, labels, slot_modality, queries, keys, values, residual, gains, up_weight, down_weight, cotangent):
    lines = dp // 2
    quarter = queries.shape[2]
    hidden_units = up_weight.shape[1]
    tokens = dp * LENGTH
    width = quarter * slots
    bf, f32 = jnp.bfloat16, jnp.float32
    any_space = pl.BlockSpec(memory_space=pl.ANY)
    scalar = pl.BlockSpec(memory_space=pltpu.SMEM)
    vm = pl.BlockSpec(memory_space=pltpu.VMEM)
    dma = pltpu.SemaphoreType.DMA
    rows_shape = (2, slots, 2, lines, LENGTH, quarter)
    chunk = width // dp
    return pl.pallas_call(
        functools.partial(layer_kernel, (lines, dp, slots, quarter, hidden_units)),
        out_shape=(
            jax.ShapeDtypeStruct((hidden_units, tokens), bf),
            jax.ShapeDtypeStruct((hidden_units, tokens), bf),
            jax.ShapeDtypeStruct(rows_shape, bf),
            jax.ShapeDtypeStruct((2, slots, LENGTH, quarter), bf),
            jax.ShapeDtypeStruct((slots, dp, 8, chunk // 8), f32),
        ),
        in_specs=[scalar, scalar] + [any_space] * 8,
        out_specs=(any_space, any_space, any_space, vm, vm),
        scratch_shapes=[
            pltpu.VMEM((slots, hidden_units, quarter), bf),
            pltpu.VMEM((slots, hidden_units, quarter), bf),
            pltpu.VMEM(rows_shape, bf),
            pltpu.VMEM((LENGTH, quarter), bf),
            pltpu.VMEM((LENGTH, quarter), bf),
            pltpu.VMEM((LENGTH, quarter), bf),
            pltpu.VMEM((LENGTH, quarter), bf),
            pltpu.VMEM(gains.shape, f32),
            pltpu.VMEM((LENGTH, quarter), bf),
            pltpu.VMEM((2, slots, LENGTH, HD), f32),
            pltpu.VMEM((dp, 8, tokens), f32),
            pltpu.VMEM((hidden_units, tokens), f32),
            pltpu.VMEM((hidden_units, tokens), f32),
            pltpu.VMEM((hidden_units, tokens), bf),
            pltpu.VMEM((hidden_units, tokens), bf),
            pltpu.VMEM((tokens, hidden_units), bf),
            pltpu.VMEM((tokens, hidden_units), bf),
            pltpu.VMEM(rows_shape, bf),
            pltpu.VMEM((2, 2, 2, lines, LENGTH, quarter), bf),
            pltpu.VMEM((2, 2, lines, LENGTH, quarter), bf),
            pltpu.VMEM((2, lines, LENGTH, quarter), bf),
            pltpu.VMEM((2, lines, LENGTH, quarter), bf),
            pltpu.VMEM((dp, 8, chunk // 8), f32),
            pltpu.VMEM((dp, 8, chunk // 8), f32),
            pltpu.VMEM((8, chunk // 8), f32),
            dma((6,)), dma((2, slots)),
            dma((dp,)), dma((dp,)),
            dma((2, slots)), dma((2, slots)),
            dma((2, lines)), dma((2, lines)),
            dma((2, lines)), dma((2, lines)),
            dma((2, 2, lines)), dma((2, 2, lines)),
            dma((2, 4)), dma((2, 4)),
            dma((2, 2)), dma((2, 2)),
            dma((2, 2)), dma((2, 2)),
            dma((2,)), dma((2,)),
            dma((2, lines)), dma((2, lines)),
            dma((2, slots)), dma((2, slots)),
            dma((dp,)), dma((dp,)),
            dma((dp,)), dma((dp,)),
            dma((slots,)), dma((slots,)),
            dma((3,)),
        ],
        compiler_params=pltpu.CompilerParams(
            collective_id=0, has_side_effects=True, vmem_limit_bytes=62 * 1024 * 1024
        ),
    )(labels, slot_modality, queries, keys, values, residual, gains, up_weight, down_weight, cotangent)


def grads_kernel(
    steps, sect_ref, modality_ref, act_ref, pre_grad_ref, rows_ref, sums_ref, gain_ref, query_ref, key_ref, value_ref,
    out_ref, res_grad_ref, query_grad_ref, key_grad_ref, value_grad_ref, up_grad_ref, down_grad_ref, gain_grad_ref,
):
    step = pl.program_id(0)
    block = rows_ref[0, 0].reshape(-1, rows_ref.shape[-1])

    @pl.when(step < steps)
    def _():
        up_grad_ref[...] = jnp.dot(
            pre_grad_ref[...], block, preferred_element_type=jnp.float32
        ).astype(jnp.bfloat16)

    @pl.when(step >= steps)
    def _():
        down_grad_ref[...] = jnp.dot(act_ref[...], block, preferred_element_type=jnp.float32).astype(jnp.bfloat16)

    @pl.when(step == 1)
    def _():
        sect = sect_ref[0]
        quarter = query_ref.shape[2]
        query, key, value = (stack_heads(ref[0]) for ref in (query_ref, key_ref, value_ref))
        attended, probs, probs_b = attend(query, key, value)
        grad = stack_heads(sums_ref[0, sect])
        value_grad = contract_first(probs_b, grad)
        dprob = contract_last(grad, value)
        delta = jnp.sum(grad.astype(jnp.float32) * attended.astype(jnp.float32), axis=-1, keepdims=True)
        dscore = (probs * (dprob - delta) * HD ** (-0.5)).astype(jnp.bfloat16)
        query_grad = jnp.dot(dscore, key, preferred_element_type=jnp.float32)
        key_grad = contract_first(dscore, query)
        for ref, grads in ((query_grad_ref, query_grad), (key_grad_ref, key_grad), (value_grad_ref, value_grad)):
            for h in range(quarter // HD):
                ref[0, :, h * HD : (h + 1) * HD] = grads[h * LENGTH : (h + 1) * LENGTH, :].astype(jnp.bfloat16)

    @pl.when(step == 2)
    def _():
        sect = sect_ref[0]
        slots, quarter = sums_ref.shape[1], sums_ref.shape[3]
        own = LENGTH // slots
        row = lax.broadcasted_iota(jnp.int32, (LENGTH, LENGTH), 0)
        col = lax.broadcasted_iota(jnp.int32, (LENGTH, LENGTH), 1)
        pick = ((row < own) & (col == row + sect * own)).astype(jnp.bfloat16)
        for a, ref in ((0, res_grad_ref), (1, out_ref)):
            for q in range(slots):
                rows = jnp.dot(pick, sums_ref[a, q], preferred_element_type=jnp.float32)
                ref[0, :, q * quarter : (q + 1) * quarter] = rows[:own, :].astype(jnp.bfloat16)
        dp, lanes = gain_ref.shape[1], gain_ref.shape[3]
        for m in range(gain_grad_ref.shape[0]):
            total = jnp.zeros(gain_ref.shape[1:], jnp.float32)
            for q in range(slots):
                total = total + jnp.where(modality_ref[q] == m, gain_ref[q], 0.0)
            for j in range(dp):
                for r in range(8):
                    first = (j * 8 + r) * lanes
                    gain_grad_ref[m : m + 1, first : first + lanes] = total[j, r : r + 1, :]


def grads(act, pre_grad, rows, sums, gain, slot_modality, queries, keys, values, width):
    hidden_units, tokens = act.shape
    _, slots, inner, lines, length, quarter = rows.shape
    bf, f32 = jnp.bfloat16, jnp.float32
    steps = slots
    sect = lax.axis_index("sect").reshape(1)
    scalar = pl.BlockSpec(memory_space=pltpu.SMEM)

    def whole(shape):
        return pl.BlockSpec(shape, lambda i: (0,) * len(shape))

    own = (1, length // slots, width)
    return pl.pallas_call(
        functools.partial(grads_kernel, steps),
        grid=(2 * steps,),
        out_shape=(
            jax.ShapeDtypeStruct(own, bf),
            jax.ShapeDtypeStruct(own, bf),
            jax.ShapeDtypeStruct(queries.shape, bf),
            jax.ShapeDtypeStruct(queries.shape, bf),
            jax.ShapeDtypeStruct(queries.shape, bf),
            jax.ShapeDtypeStruct((hidden_units, width), bf),
            jax.ShapeDtypeStruct((hidden_units, width), bf),
            jax.ShapeDtypeStruct((MODALITIES, width), f32),
        ),
        in_specs=[
            scalar,
            scalar,
            whole(act.shape),
            whole(act.shape),
            pl.BlockSpec(
                (1, 1, inner, lines, length, quarter),
                lambda i: (jnp.where(i < steps, 1, 0), jnp.where(i < steps, i, i - steps), 0, 0, 0, 0),
            ),
            whole(sums.shape),
            whole(gain.shape),
            whole(queries.shape),
            whole(queries.shape),
            whole(queries.shape),
        ],
        out_specs=(
            whole(own),
            whole(own),
            whole(queries.shape),
            whole(queries.shape),
            whole(queries.shape),
            pl.BlockSpec((hidden_units, quarter), lambda i: (0, jnp.minimum(i, steps - 1))),
            pl.BlockSpec((hidden_units, quarter), lambda i: (0, jnp.maximum(i - steps, 0))),
            whole((MODALITIES, width)),
        ),
        compiler_params=pltpu.CompilerParams(
            dimension_semantics=("arbitrary",), vmem_limit_bytes=VMEM_BYTES
        ),
    )(sect, slot_modality, act, pre_grad, rows, sums, gain, queries, keys, values)


def fast_on_device(
    dp, slots, queries, keys, values, residual, labels, slot_modality, gains, up_weight, down_weight, cotangent
):
    act, pre_grad, rows, sums, gain = layer(
        dp, slots, labels, slot_modality, queries, keys, values, residual, gains, up_weight, down_weight, cotangent
    )
    output, residual_grad, query_grad, key_grad, value_grad, up_grad, down_grad, gain_grad = grads(
        act, pre_grad, rows, sums, gain, slot_modality, queries, keys, values, residual.shape[2]
    )
    return (
        output, residual_grad, query_grad, key_grad, value_grad, up_grad[None], down_grad[None], gain_grad,
    )


def solution(mesh):
    in_specs = (
        P("dp", None, "sect"),
        P("dp", None, "sect"),
        P("dp", None, "sect"),
        P("dp", None, None),
        P("dp", None),
        P(),
        P(),
        P("sect", "dp", None),
        P("sect", "dp", None),
        P("dp", None, None),
    )
    out_specs = (
        P("dp", "sect", None),
        P("dp", "sect", None),
        P("dp", None, "sect"),
        P("dp", None, "sect"),
        P("dp", None, "sect"),
        P("sect", "dp", None),
        P("sect", "dp", None),
        P(),
    )
    dp, slots = mesh.shape["dp"], mesh.shape["sect"]
    body = functools.partial(fast_on_device if (dp, slots) == (8, 4) else on_device, dp, slots)
    return jax.shard_map(
        body, mesh=mesh, in_specs=in_specs, out_specs=out_specs, check_vma=False
    )
```

```python
import functools

import jax
import jax.numpy as jnp
from jax import lax
from jax.experimental import pallas as pl
from jax.experimental.pallas import tpu as pltpu
from jax.sharding import PartitionSpec as P

HD = 128
MODALITIES = 3


def causal_forward(queries, keys, values):
    seq_count, length, width = queries.shape
    head_count = width // HD
    query_f = queries.astype(jnp.float32).reshape(seq_count, length, head_count, HD)
    key_f = keys.astype(jnp.float32).reshape(seq_count, length, head_count, HD)
    value_f = values.astype(jnp.float32).reshape(seq_count, length, head_count, HD)
    scores = jnp.einsum("sqhd,skhd->shqk", query_f, key_f) * HD ** (-0.5)
    position = jnp.arange(length)
    causal = position[:, None] >= position[None, :]
    scores = jnp.where(causal, scores, -1e30)
    probs = jax.nn.softmax(scores, axis=-1)
    probs_b = probs.astype(jnp.bfloat16)
    attended = jnp.einsum("shqk,skhd->sqhd", probs_b.astype(jnp.float32), value_f)
    return (attended.astype(jnp.bfloat16).reshape(seq_count, length, width), probs, probs_b)


def causal_backward(grad_out, queries, keys, values, attended, probs, probs_b):
    seq_count, length, width = queries.shape
    head_count = width // HD
    shape = (seq_count, length, head_count, HD)
    grad_f = grad_out.astype(jnp.float32).reshape(shape)
    query_f = queries.astype(jnp.float32).reshape(shape)
    key_f = keys.astype(jnp.float32).reshape(shape)
    value_f = values.astype(jnp.float32).reshape(shape)
    attended_f = attended.astype(jnp.float32).reshape(shape)
    value_grad = jnp.einsum("shqk,sqhd->skhd", probs_b.astype(jnp.float32), grad_f).astype(
        jnp.bfloat16
    )
    dprob = jnp.einsum("sqhd,skhd->shqk", grad_f, value_f)
    delta = jnp.einsum("sqhd,sqhd->shq", grad_f, attended_f)
    dscore = (
        (probs * (dprob - delta[..., None]) * HD ** (-0.5)).astype(jnp.bfloat16).astype(jnp.float32)
    )
    query_grad = jnp.einsum("shqk,skhd->sqhd", dscore, key_f).astype(jnp.bfloat16)
    key_grad = jnp.einsum("shqk,sqhd->skhd", dscore, query_f).astype(jnp.bfloat16)
    return (
        query_grad.reshape(seq_count, length, width),
        key_grad.reshape(seq_count, length, width),
        value_grad.reshape(seq_count, length, width),
    )


MESH = pl.DeviceIdType.MESH
VMEM_BYTES = 60 * 1024 * 1024


def remote(src, dst, send_sem, recv_sem, dp_index, sect_index):
    return pltpu.make_async_remote_copy(
        src_ref=src,
        dst_ref=dst,
        send_sem=send_sem,
        recv_sem=recv_sem,
        device_id=(dp_index, sect_index),
        device_id_type=MESH,
    )


def greet(peers):
    barrier = pltpu.get_barrier_semaphore()
    total = jnp.int32(0)
    for dp_index, sect_index, present in peers:
        if present is None:
            pl.semaphore_signal(barrier, inc=1, device_id=(dp_index, sect_index), device_id_type=MESH)
            total = total + 1
        else:

            @pl.when(present)
            def _():
                pl.semaphore_signal(
                    barrier, inc=1, device_id=(dp_index, sect_index), device_id_type=MESH
                )

            total = total + present.astype(jnp.int32)
    pl.semaphore_wait(barrier, total)


class LineGather:
    def __init__(self, buf, sems, lines, slot):
        self.buf, self.lines = buf, lines
        self.send_sems, self.recv_sems = sems
        self.slot = slot
        self.me = lax.axis_index("dp")
        self.sect = lax.axis_index("sect")
        self.outer, self.inner = self.me // 2, self.me % 2

    def copy(self, way, outer, target, incoming=False):
        inner = (1 - self.inner) if (incoming and way == 2) else self.inner
        block = self.buf.at[outer * 2 + inner]
        recv = 1 if way == 2 else 0
        return remote(
            block,
            block,
            self.send_sems.at[self.slot, way, outer],
            self.recv_sems.at[self.slot, recv, outer],
            target,
            self.sect,
        )

    def pass_up(self, outer):
        return self.copy(0, outer, jnp.minimum(self.outer + 1, self.lines - 1) * 2 + self.inner)

    def pass_down(self, outer):
        return self.copy(1, outer, jnp.maximum(self.outer - 1, 0) * 2 + self.inner)

    def pass_across(self, outer):
        return self.copy(2, outer, self.outer * 2 + 1 - self.inner)

    def start(self):
        outer = self.outer

        @pl.when(outer + 1 < self.lines)
        def _():
            self.pass_up(outer).start()

        @pl.when(outer > 0)
        def _():
            self.pass_down(outer).start()

        self.pass_across(outer).start()

    def relay(self, step):
        outer = self.outer

        @pl.when(outer - step >= 0)
        def _():
            block = outer - step
            self.pass_down(block).wait_recv()

            @pl.when(outer + 1 < self.lines)
            def _():
                self.pass_up(block).start()

            self.pass_across(block).start()

        @pl.when(outer + step < self.lines)
        def _():
            block = outer + step
            self.pass_up(block).wait_recv()

            @pl.when(outer > 0)
            def _():
                self.pass_down(block).start()

            self.pass_across(block).start()

    def finish(self):
        outer = self.outer
        for block in range(self.lines):
            self.copy(2, block, self.outer * 2 + 1 - self.inner, incoming=True).wait_recv()
            self.pass_across(block).wait_send()

            @pl.when((outer + 1 < self.lines) & (block <= outer))
            def _():
                self.pass_up(block).wait_send()

            @pl.when((outer > 0) & (block >= outer))
            def _():
                self.pass_down(block).wait_send()


def front_kernel(
    lines, slots, att_ref, res_ref, gain_ref, sel_ref, cot_ref, hidden_ref, norm_ref, rows_ref, cots_ref,
    att_all, send_sems, recv_sems, att_send, att_recv,
):
    me, sect = lax.axis_index("dp"), lax.axis_index("sect")
    outer, inner = me // 2, me % 2
    width = att_ref.shape[1]
    peers = [(me, lax.rem(sect + k, slots), None) for k in range(1, slots)]
    peers.append((outer * 2 + 1 - inner, sect, None))
    peers.append((jnp.minimum(outer + 1, lines - 1) * 2 + inner, sect, outer + 1 < lines))
    peers.append((jnp.maximum(outer - 1, 0) * 2 + inner, sect, outer > 0))
    sel = sel_ref[...]
    cots_ref[me] = jnp.dot(sel, cot_ref[...], preferred_element_type=jnp.float32).astype(jnp.bfloat16)
    greet(peers)
    copies = []
    for k in range(1, slots):
        target = lax.rem(sect + k, slots)
        copies.append(
            remote(att_ref, att_all.at[sect], att_send.at[k], att_recv.at[sect], me, target)
        )
        copies[-1].start()
    cots = LineGather(cots_ref, (send_sems, recv_sems), lines, 0)
    rows = LineGather(rows_ref, (send_sems, recv_sems), lines, 1)
    cots.start()
    att_all[sect] = att_ref[...]
    for k in range(1, slots):
        source = lax.rem(sect + k, slots)
        remote(att_ref, att_all.at[source], att_send.at[k], att_recv.at[source], me, source).wait_recv()
    square = jnp.zeros((res_ref.shape[0], 1), jnp.float32)
    for block in range(slots):
        cols = slice(block * width, (block + 1) * width)
        hid = (
            res_ref[:, cols].astype(jnp.float32) + att_all[block].astype(jnp.float32)
        ).astype(jnp.bfloat16)
        hidden_ref[:, cols] = hid
        hid_f = hid.astype(jnp.float32)
        square = square + jnp.sum(hid_f * hid_f, axis=-1, keepdims=True)
    inverse = lax.rsqrt(square / (slots * width) + 1e-05)
    norm_ref[...] = jnp.broadcast_to(inverse, norm_ref.shape)
    for block in range(slots):
        cols = slice(block * width, (block + 1) * width)
        normed = (hidden_ref[:, cols].astype(jnp.float32) * inverse * gain_ref[:, cols]).astype(
            jnp.bfloat16
        )
        rows_ref[me, :, cols] = jnp.dot(sel, normed, preferred_element_type=jnp.float32).astype(
            jnp.bfloat16
        )
    rows.start()
    for step in range(1, lines):
        cots.relay(step)
        rows.relay(step)
    cots.finish()
    rows.finish()
    for one in copies:
        one.wait_send()


def front(att, residual, gain_rows, selector, cotangent, dp, slots):
    length, width = residual.shape
    capacity = selector.shape[0]
    vm = pl.BlockSpec(memory_space=pltpu.VMEM)
    return pl.pallas_call(
        functools.partial(front_kernel, dp // 2, slots),
        out_shape=(
            jax.ShapeDtypeStruct((length, width), jnp.bfloat16),
            jax.ShapeDtypeStruct((length, 128), jnp.float32),
            jax.ShapeDtypeStruct((dp, capacity, width), jnp.bfloat16),
            jax.ShapeDtypeStruct((dp, capacity, width), jnp.bfloat16),
        ),
        in_specs=[vm] * 5,
        out_specs=(vm,) * 4,
        scratch_shapes=[
            pltpu.VMEM((slots,) + att.shape, jnp.bfloat16),
            pltpu.SemaphoreType.DMA((2, 3, dp // 2)),
            pltpu.SemaphoreType.DMA((2, 2, dp // 2)),
            pltpu.SemaphoreType.DMA((slots,)),
            pltpu.SemaphoreType.DMA((slots,)),
        ],
        compiler_params=pltpu.CompilerParams(
            collective_id=0, has_side_effects=True, vmem_limit_bytes=VMEM_BYTES
        ),
    )(att, residual, gain_rows, selector, cotangent)


def ffn_kernel(tail, rows_ref, cots_ref, up_ref, down_ref, out_ref, back_ref, upg_ref, downg_ref, out_acc, back_acc):
    step = pl.program_id(0)
    last = pl.num_programs(0) - 1
    full = up_ref.shape[0]

    @pl.when(step == 0)
    def _():
        out_acc[...] = jnp.zeros_like(out_acc)
        back_acc[...] = jnp.zeros_like(back_acc)

    def run(size):
        rows, cots = rows_ref[...], cots_ref[...]
        preact = contract_last(rows, up_ref[:size, :])
        back = contract_last(cots, down_ref[:size, :])
        sigma = jax.nn.sigmoid(preact)
        activated = (preact * sigma).astype(jnp.bfloat16)
        pre_grad = (back * sigma * (1.0 + preact * (1.0 - sigma))).astype(jnp.bfloat16)
        out_acc[...] += jnp.dot(activated, down_ref[:size, :], preferred_element_type=jnp.float32)
        back_acc[...] += jnp.dot(pre_grad, up_ref[:size, :], preferred_element_type=jnp.float32)
        downg_ref[:size, :] = contract_first(activated, cots).astype(jnp.bfloat16)
        upg_ref[:size, :] = contract_first(pre_grad, rows).astype(jnp.bfloat16)

    if tail == full:
        run(full)
    else:

        @pl.when(step < last)
        def _():
            run(full)

        @pl.when(step == last)
        def _():
            run(tail)

    @pl.when(step == last)
    def _():
        out_ref[...] = out_acc[...].astype(jnp.bfloat16)
        back_ref[...] = back_acc[...].astype(jnp.bfloat16)


def ffn(rows, cots, up, down):
    count, width = rows.shape
    hidden_units = up.shape[0]
    chunk = min(256 if count <= 128 else 128, hidden_units)
    steps = pl.cdiv(hidden_units, chunk)
    tail = hidden_units - (steps - 1) * chunk
    whole = pl.BlockSpec((count, width), lambda i: (0, 0))
    weight = pl.BlockSpec((chunk, width), lambda i: (i, 0))
    return pl.pallas_call(
        functools.partial(ffn_kernel, tail),
        grid=(steps,),
        out_shape=(
            jax.ShapeDtypeStruct((count, width), jnp.bfloat16),
            jax.ShapeDtypeStruct((count, width), jnp.bfloat16),
            jax.ShapeDtypeStruct(up.shape, jnp.bfloat16),
            jax.ShapeDtypeStruct(down.shape, jnp.bfloat16),
        ),
        in_specs=[whole, whole, weight, weight],
        out_specs=(whole, whole, weight, weight),
        scratch_shapes=[
            pltpu.VMEM((count, width), jnp.float32),
            pltpu.VMEM((count, width), jnp.float32),
        ],
        compiler_params=pltpu.CompilerParams(
            dimension_semantics=("arbitrary",), vmem_limit_bytes=VMEM_BYTES
        ),
    )(rows, cots, up, down)


def reduce_kernel(lines, slots, out_in, back_in, sums_ref, from_pair, pair_sum, from_line, pair_send, pair_recv,
                  line_send, line_recv, sect_send, sect_recv):
    me, sect = lax.axis_index("dp"), lax.axis_index("sect")
    outer, inner = me // 2, me % 2
    partner = outer * 2 + 1 - inner
    terms = (back_in, out_in)
    peers = [(me, lax.rem(sect + k, slots), None) for k in range(1, slots)]
    peers.append((partner, sect, None))
    for k in range(1, lines):
        peers.append((lax.rem(outer + k, lines) * 2 + inner, sect, None))
    greet(peers)
    order = [(k, step) for k in range(2) for step in list(range(1, lines)) + [0]]

    def across(k, step):
        line = lax.rem(outer + step, lines)
        return remote(
            terms[k].at[line * 2 + 1 - inner],
            from_pair.at[k, step],
            pair_send.at[k, step],
            pair_recv.at[k, step],
            partner,
            sect,
        )

    def along(k, step):
        line = lax.rem(outer + step, lines)
        return remote(
            pair_sum.at[k, step],
            from_line.at[k, step],
            line_send.at[k, step],
            line_recv.at[k, step],
            line * 2 + inner,
            sect,
        )

    def to_sect(k, hop):
        target = lax.rem(sect + hop, slots)
        return remote(
            sums_ref.at[k, sect],
            sums_ref.at[k, sect],
            sect_send.at[k, hop],
            sect_recv.at[k, sect],
            me,
            target,
        )

    def from_sect(k, hop):
        source = lax.rem(sect + hop, slots)
        return remote(
            sums_ref.at[k, source],
            sums_ref.at[k, source],
            sect_send.at[k, hop],
            sect_recv.at[k, source],
            me,
            source,
        )

    for k, step in order:
        across(k, step).start()
    for k in range(2):
        for step in list(range(1, lines)) + [0]:
            across(k, step).wait_recv()
            line = lax.rem(outer + step, lines)
            own = terms[k][line * 2 + inner].astype(jnp.float32) + from_pair[k, step].astype(jnp.float32)
            if step:
                pair_sum[k, step] = own.astype(jnp.bfloat16)
                along(k, step).start()
        for step in range(1, lines):
            along(k, step).wait_recv()
            own = own + from_line[k, step].astype(jnp.float32)
        sums_ref[k, sect] = own.astype(jnp.bfloat16)
        for hop in range(1, slots):
            to_sect(k, hop).start()
    for k in range(2):
        for hop in range(1, slots):
            from_sect(k, hop).wait_recv()
            to_sect(k, hop).wait_send()
        for step in range(lines):
            across(k, step).wait_send()
            if step:
                along(k, step).wait_send()


def reduce_terms(out_terms, back_terms, slots):
    dp, capacity, width = out_terms.shape
    lines = dp // 2
    vm = pl.BlockSpec(memory_space=pltpu.VMEM)
    dma = pltpu.SemaphoreType.DMA
    return pl.pallas_call(
        functools.partial(reduce_kernel, lines, slots),
        out_shape=jax.ShapeDtypeStruct((2, slots, capacity, width), jnp.bfloat16),
        in_specs=[vm] * 2,
        out_specs=vm,
        scratch_shapes=[
            pltpu.VMEM((2, lines, capacity, width), jnp.bfloat16),
            pltpu.VMEM((2, lines, capacity, width), jnp.bfloat16),
            pltpu.VMEM((2, lines, capacity, width), jnp.bfloat16),
            dma((2, lines)),
            dma((2, lines)),
            dma((2, lines)),
            dma((2, lines)),
            dma((2, slots)),
            dma((2, slots)),
        ],
        compiler_params=pltpu.CompilerParams(
            collective_id=1, has_side_effects=True, vmem_limit_bytes=VMEM_BYTES
        ),
    )(out_terms, back_terms)


def gain_kernel(dp, slots, part_ref, total_ref, inbox, mine, first_send, first_recv, next_send, next_recv, sect_send, sect_recv):
    me, sect = lax.axis_index("dp"), lax.axis_index("sect")
    peers = [(me, lax.rem(sect + k, slots), None) for k in range(1, slots)]
    peers += [(lax.rem(me + k, dp), sect, None) for k in range(1, dp)]
    greet(peers)

    def scatter(k):
        target = lax.rem(me + k, dp)
        return remote(
            part_ref.at[sect, target], inbox.at[k], first_send.at[k], first_recv.at[k], target, sect
        )

    def spread_sum(k):
        target = lax.rem(me + k, dp)
        return remote(
            mine, total_ref.at[sect, me], next_send.at[k], next_recv.at[k], target, sect
        )

    def to_sect(k):
        return remote(
            total_ref.at[sect],
            total_ref.at[sect],
            sect_send.at[k],
            sect_recv.at[k],
            me,
            lax.rem(sect + k, slots),
        )

    for k in range(1, dp):
        scatter(k).start()
    total = part_ref[sect, me]
    for k in range(1, dp):
        scatter(k).wait_recv()
        total = total + inbox[k]
    mine[...] = total
    for k in range(1, dp):
        spread_sum(k).start()
    total_ref[sect, me] = total
    for k in range(1, dp):
        spread_sum(k).wait_recv()
    for k in range(1, slots):
        to_sect(k).start()
    for k in range(1, slots):
        to_sect(k).wait_recv()
        to_sect(k).wait_send()
    for k in range(1, dp):
        scatter(k).wait_send()
        spread_sum(k).wait_send()


def gain_sum(part, dp, slots):
    kinds, width = part.shape
    cols = width // (dp * slots)
    padded = jnp.concatenate([part, jnp.zeros((8 - kinds, width), part.dtype)], 0)
    pieces = padded.reshape(8, slots, dp, cols).transpose(1, 2, 0, 3)
    vm = pl.BlockSpec(memory_space=pltpu.VMEM)
    dma = pltpu.SemaphoreType.DMA
    total = pl.pallas_call(
        functools.partial(gain_kernel, dp, slots),
        out_shape=jax.ShapeDtypeStruct(pieces.shape, pieces.dtype),
        in_specs=[vm],
        out_specs=vm,
        scratch_shapes=[
            pltpu.VMEM((dp, 8, cols), pieces.dtype),
            pltpu.VMEM((8, cols), pieces.dtype),
            dma((dp,)),
            dma((dp,)),
            dma((dp,)),
            dma((dp,)),
            dma((slots,)),
            dma((slots,)),
        ],
        compiler_params=pltpu.CompilerParams(collective_id=2, has_side_effects=True),
    )(pieces)
    return total.transpose(2, 0, 1, 3).reshape(8, width)[:kinds]


def contract_last(left, right):
    return lax.dot_general(
        left, right, (((1,), (1,)), ((), ())), preferred_element_type=jnp.float32
    )


def contract_first(left, right):
    return lax.dot_general(
        left, right, (((0,), (0,)), ((), ())), preferred_element_type=jnp.float32
    )


def selectors(token_labels, slot_modality):
    length = token_labels.shape[0]
    keep = token_labels[None, :] == slot_modality[:, None]
    upto = jnp.arange(length)[None, :] <= jnp.arange(length)[:, None]
    rank = jnp.sum((keep[:, None, :] & upto[None]).astype(jnp.int32), axis=2) - 1
    capacity = length // 2
    return (rank[:, None, :] == jnp.arange(capacity)[None, :, None]) & keep[:, None, :]


def on_device(
    dp, slots, queries, keys, values, residual, labels, slot_modality, gains, up_weight, down_weight, cotangent
):
    attended_block, probs, probs_b = causal_forward(queries, keys, values)
    token_labels = labels[0]
    onehot = (token_labels[:, None] == jnp.arange(MODALITIES)[None, :]).astype(jnp.float32)
    gain_rows = jnp.dot(onehot, gains, precision=lax.Precision.HIGHEST)
    slot_index = lax.axis_index("sect")
    all_select = selectors(token_labels, slot_modality).astype(jnp.bfloat16)
    selector = lax.dynamic_index_in_dim(all_select, slot_index, 0, keepdims=False)
    capacity, length = selector.shape
    grad_full = cotangent[0]
    hidden, inverse, rows, cots = front(
        attended_block[0], residual[0], gain_rows, selector, grad_full, dp, slots
    )
    width = hidden.shape[1]
    inverse = inverse[:, :1]
    hidden_f = hidden.astype(jnp.float32)
    normed_f = hidden_f * inverse
    out_terms, back_terms, up_grad, down_grad = ffn(
        rows.reshape(-1, width), cots.reshape(-1, width), up_weight[0], down_weight[0]
    )
    sums = reduce_terms(
        out_terms.reshape(dp, capacity, width), back_terms.reshape(dp, capacity, width), slots
    ).reshape(2, slots * capacity, width)
    place = all_select.reshape(slots * capacity, length)
    norm_grad = contract_first(place, sums[0])
    quarter = length // slots
    place_own = lax.dynamic_slice_in_dim(place, slot_index * quarter, quarter, 1)
    hidden_own = lax.dynamic_slice_in_dim(hidden_f, slot_index * quarter, quarter, 0)
    output = (hidden_own + contract_first(place_own, sums[1])).astype(jnp.bfloat16)[None]
    scaled = norm_grad * gain_rows
    hidden_grad = grad_full.astype(jnp.float32) + inverse * (
        scaled - normed_f * jnp.mean(scaled * normed_f, axis=-1, keepdims=True)
    )
    residual_full = hidden_grad.astype(jnp.bfloat16)
    residual_grad = lax.dynamic_slice_in_dim(residual_full, slot_index * quarter, quarter, 0)[None]
    gain_part = jnp.dot(onehot.T, norm_grad * normed_f, precision=lax.Precision.HIGHEST)
    gain_grad = gain_sum(gain_part, dp, slots)
    block_width = queries.shape[2]
    grad_block = lax.dynamic_slice_in_dim(residual_full, slot_index * block_width, block_width, 1)[
        None
    ]
    query_grad, key_grad, value_grad = causal_backward(
        grad_block, queries, keys, values, attended_block, probs, probs_b
    )
    return (
        output, residual_grad, query_grad, key_grad, value_grad, up_grad[None], down_grad[None], gain_grad,
    )


def flip(index, offset):
    bit = 1
    while bit <= offset:
        if offset & bit:
            index = index + bit - 2 * bit * (lax.div(index, bit) % 2)
        bit *= 2
    return index


def block_mask(rows):
    row = lax.broadcasted_iota(jnp.int32, (rows, rows), 0)
    col = lax.broadcasted_iota(jnp.int32, (rows, rows), 1)
    return (row // LENGTH == col // LENGTH) & (col <= row)


def stack_heads(block):
    heads = block.shape[1] // HD
    return jnp.concatenate([block[:, h * HD : (h + 1) * HD] for h in range(heads)], axis=0)


def attend(query, key, value):
    scores = contract_last(query, key) * HD ** (-0.5)
    scores = jnp.where(block_mask(query.shape[0]), scores, -1e30)
    top = jnp.max(scores, axis=-1, keepdims=True)
    weight = jnp.exp(scores - top)
    probs = weight / jnp.sum(weight, axis=-1, keepdims=True)
    probs_b = probs.astype(jnp.bfloat16)
    attended = jnp.dot(probs_b, value, preferred_element_type=jnp.float32).astype(jnp.bfloat16)
    return attended, probs, probs_b


def layer_kernel(
    dims, labels_ref, modality_ref, query_hbm, key_hbm, value_hbm, residual_hbm, gains_hbm, up_hbm, down_hbm, cot_hbm,
    act_out, pre_grad_out, rows_out, sums_ref, gain_ref, heads_ref,
    up_w, down_w, rows_all, query_s, key_s, value_s, residual_s, gains_s, hidden_s, attended_s, probs_s, probs_b_s, packed,
    stat, tags, pre_t, back_t,
    act_t, pre_grad_t, act_n, pre_grad_n, parts, from_core, from_second, from_first, from_line, gain_mine, gain_inbox,
    gain_own, load_sem, weight_sem, tag_send, tag_recv, stat_send, stat_recv, line_send, line_recv, first_send, first_recv,
    second_send, second_recv, core_send, core_recv, r1_send, r1_recv, r2_send, r2_recv, r3_send, r3_recv,
    r4_send, r4_recv, spread_send, spread_recv, gs_send, gs_recv, gd_send, gd_recv, gx_send, gx_recv, store_sem,
):
    lines, dp, slots, quarter, hidden_units = dims
    width = quarter * slots
    d, s = lax.axis_index("dp"), lax.axis_index("sect")
    line, inner = lax.div(d, 2), d % 2
    y, c = lax.div(s, 2), s % 2
    tokens = dp * LENGTH

    core_id = (d, flip(s, 1))
    turn = [c, 1 - c]
    first_id = [(d + (1 - t) * (1 - 2 * inner), s + t * 2 * (1 - 2 * y)) for t in turn]
    second_id = [first_id[1], first_id[0]]

    def send(src, dst, send_sem, recv_sem, target):
        return remote(src, dst, send_sem, recv_sem, target[0], target[1])

    def line_id(k):
        return (flip(line, k) * 2 + inner, s)

    def side(a, far_first, far_second):
        dy = far_second * (1 - turn[a]) + far_first * turn[a]
        di = far_first * (1 - turn[a]) + far_second * turn[a]
        return y + dy * (1 - 2 * y), inner + di * (1 - 2 * inner), dy * 2 + di

    mine = rows_all.at[0, s, inner, line]
    loads = [
        pltpu.make_async_copy(cot_hbm.at[0, :, pl.ds(pl.multiple_of(s * quarter, quarter), quarter)], mine, load_sem.at[0]),
        pltpu.make_async_copy(query_hbm.at[0], query_s, load_sem.at[1]),
        pltpu.make_async_copy(key_hbm.at[0], key_s, load_sem.at[2]),
        pltpu.make_async_copy(value_hbm.at[0], value_s, load_sem.at[3]),
        pltpu.make_async_copy(
            residual_hbm.at[0, :, pl.ds(pl.multiple_of(s * quarter, quarter), quarter)], residual_s, load_sem.at[4]
        ),
        pltpu.make_async_copy(gains_hbm, gains_s, load_sem.at[5]),
    ]
    for one in loads:
        one.start()
    order = [y * 2, y * 2 + 1, (1 - y) * 2, (1 - y) * 2 + 1]

    def weight_load(which, step):
        src, dst = ((down_hbm, down_w), (up_hbm, up_w))[which]
        at = order[step]
        return pltpu.make_async_copy(
            src.at[0, :, pl.ds(pl.multiple_of(at * quarter, quarter), quarter)], dst.at[at], weight_sem.at[which, step]
        )

    for step in range(slots):
        weight_load(0, step).start()

    lane = lax.broadcasted_iota(jnp.int32, (8, tokens), 1)
    sub = lax.broadcasted_iota(jnp.int32, (LENGTH, HD), 0)
    base = (inner * lines + line) * LENGTH
    tag = jnp.zeros((8, tokens), jnp.float32)
    own_tag = jnp.zeros((LENGTH, HD), jnp.float32)
    for t in range(LENGTH):
        value = labels_ref[0, t].astype(jnp.float32)
        tag = jnp.where(lane == base + t, value, tag)
        own_tag = jnp.where(sub == t, value, own_tag)
    tags[0] = tag

    barrier = pltpu.get_barrier_semaphore()
    for k in range(1, dp):
        pl.semaphore_signal(barrier, inc=1, device_id=(flip(d, k), s), device_id_type=MESH)
    for k in range(1, slots):
        pl.semaphore_signal(barrier, inc=1, device_id=(d, flip(s, k)), device_id_type=MESH)

    def on_line(a, k, where):
        block = rows_all.at[a, s, inner, where]
        return send(block, block, line_send.at[a, k], line_recv.at[a, k], line_id(k))

    def on_first(a, k):
        block = rows_all.at[a, s, inner, flip(line, k)]
        return send(block, block, first_send.at[a, k], first_recv.at[a, k], first_id[a])

    def on_second(a, f, k):
        gy, gi, _ = side(a, f, 0)
        block = rows_all.at[a, gy * 2 + c, gi, flip(line, k)]
        return send(block, block, second_send.at[a, f, k], second_recv.at[a, f, k], second_id[a])

    def on_core(a, f, g):
        gy, gi, place = side(a, f, g)
        group = rows_all.at[a, gy * 2 + c, gi]
        return send(group, group, core_send.at[a, place], core_recv.at[a, place], core_id)

    def gather_start(a):
        for k in range(1, lines):
            on_line(a, k, line).start()
        on_first(a, 0).start()
        on_second(a, 0, 0).start()

    def gather_line(a, k):
        on_line(a, k, line).wait_recv()
        on_first(a, k).start()
        on_second(a, 0, k).start()
        if k == lines - 1:
            on_core(a, 0, 0).start()

    def gather_first(a, k):
        on_first(a, k).wait_recv()
        on_second(a, 1, k).start()
        if k == lines - 1:
            on_core(a, 1, 0).start()

    def gather_second(a, f):
        for k in range(lines):
            on_second(a, f, k).wait_recv()
        on_core(a, f, 1).start()

    def gather_core(a, dy):
        for di in range(2):
            group = rows_all.at[a, 0, 0]
            send(group, group, core_send.at[a, dy * 2 + di], core_recv.at[a, dy * 2 + di], core_id).wait_recv()

    def gather_end(a):
        for k in range(1, lines):
            on_line(a, k, line).wait_send()
        for k in range(lines):
            on_first(a, k).wait_send()
            for f in range(2):
                on_second(a, f, k).wait_send()
        for f in range(2):
            for g in range(2):
                on_core(a, f, g).wait_send()

    def send_tag(k):
        return send(tags.at[0], tags.at[k], tag_send.at[k], tag_recv.at[k], (flip(d, k), s))

    def send_stat(turn, k):
        return send(stat.at[turn, 0], stat.at[turn, k], stat_send.at[turn, k], stat_recv.at[turn, k], (d, flip(s, k)))

    for one in loads:
        one.wait()
    attended, probs, probs_b = attend(stack_heads(query_s[...]), stack_heads(key_s[...]), stack_heads(value_s[...]))
    attended_s[...] = attended
    probs_s[...] = probs
    probs_b_s[...] = probs_b
    square = jnp.zeros((LENGTH, 1), jnp.float32)
    for h in range(quarter // HD):
        cols = slice(h * HD, (h + 1) * HD)
        hid = (
            residual_s[:, cols].astype(jnp.float32) + attended[h * LENGTH : (h + 1) * LENGTH, :].astype(jnp.float32)
        ).astype(jnp.bfloat16)
        hidden_s[:, cols] = hid
        hid_f = hid.astype(jnp.float32)
        square = square + jnp.sum(hid_f * hid_f, axis=-1, keepdims=True)
    stat[0, 0] = jnp.broadcast_to(square, (LENGTH, HD))
    pl.semaphore_wait(barrier, dp - 1 + slots - 1)
    for k in range(1, slots):
        send_stat(0, k).start()
    gather_start(0)
    for k in range(1, dp):
        send_tag(k).start()
    for k in range(1, slots):
        send_stat(0, k).wait_recv()
    total = (stat[0, 0] + stat[0, 1] + stat[0, 2] + stat[0, 3])[:, :1]
    inverse = lax.rsqrt(total / width + 1e-05)

    def gain_rows():
        g = gains_s[:, pl.ds(pl.multiple_of(s * quarter, quarter), quarter)]
        own = own_tag[:, :1]
        return jnp.where(own == 0.0, g[0:1, :], jnp.where(own == 1.0, g[1:2, :], g[2:3, :]))

    rows_all[1, s, inner, line] = (hidden_s[...].astype(jnp.float32) * inverse * gain_rows()).astype(jnp.bfloat16)
    gather_start(1)
    gather_first(0, 0)
    weight_load(1, 0).start()
    for k in range(1, lines):
        gather_line(0, k)
    gather_first(1, 0)
    weight_load(1, 1).start()
    for k in range(1, lines):
        gather_first(0, k)
        gather_line(1, k)
    weight_load(1, 2).start()

    half = hidden_units // 2

    def project(a, step, parts=(0, 1)):
        dst, weight = ((back_t, down_w), (pre_t, up_w))[a]
        at = order[step]
        if 0 in parts:
            weight_load(a, step).wait()
        block = rows_all[a, at].reshape(tokens, quarter)
        for h in [half * part for part in parts]:
            term = contract_last(weight[at, h : h + half, :], block)
            if step == 0:
                dst[h : h + half, :] = term
            else:
                dst[h : h + half, :] += term

    gather_second(0, 0)
    gather_core(0, 0)
    project(0, 0, (0,))
    gather_first(1, 1)
    project(0, 0, (1,))
    gather_first(1, 2)
    project(0, 1, (0,))
    for k in range(3, lines):
        gather_first(1, k)
    weight_load(1, 3).start()
    project(0, 1, (1,))
    gather_second(0, 1)
    gather_core(0, 1)
    project(0, 2)
    gather_second(1, 0)
    project(0, 3)
    gather_core(1, 0)
    project(1, 0)
    gather_second(1, 1)
    project(1, 1)
    gather_core(1, 1)
    project(1, 2)
    project(1, 3)
    keep_rows = pltpu.make_async_copy(rows_all, rows_out, store_sem.at[0])
    keep_rows.start()

    for k in range(1, dp):
        send_tag(k).wait_recv()
    all_tags = tags[0]
    for k in range(1, dp):
        all_tags = all_tags + tags[k]
    modality = modality_ref[s].astype(jnp.float32)
    keep = all_tags[:1, :] == modality
    preact = pre_t[...]
    sigma = jax.nn.sigmoid(preact)
    pre_grad = jnp.where(keep, back_t[...] * sigma * (1.0 + preact * (1.0 - sigma)), 0.0)
    pre_grad_t[...] = pre_grad.astype(jnp.bfloat16)
    pre_grad_n[...] = pre_grad.T.astype(jnp.bfloat16)
    keep_act = pltpu.make_async_copy(act_t, act_out, store_sem.at[1])
    keep_pre_grad = pltpu.make_async_copy(pre_grad_t, pre_grad_out, store_sem.at[2])
    keep_pre_grad.start()

    def to_core(a, dy):
        gy = y + dy * (1 - 2 * y)
        return send(parts.at[a, gy * 2 + 1 - c], from_core.at[a, dy], r1_send.at[a, dy], r1_recv.at[a, dy], core_id)

    def to_second(a, f, k):
        gy, gi, _ = side(a, f, 1)
        block = parts.at[a, gy * 2 + c, gi, flip(line, k)]
        return send(block, from_second.at[a, f, k], r2_send.at[a, f, k], r2_recv.at[a, f, k], second_id[a])

    def to_first(a, k):
        gy, gi, _ = side(a, 1, 0)
        block = parts.at[a, gy * 2 + c, gi, flip(line, k)]
        return send(block, from_first.at[a, k], r3_send.at[a, k], r3_recv.at[a, k], first_id[a])

    def to_line(a, k):
        block = parts.at[a, s, inner, flip(line, k)]
        return send(block, from_line.at[a, k], r4_send.at[a, k], r4_recv.at[a, k], line_id(k))

    def partial_sum(a, at):
        source, weight = ((pre_grad_n, up_w), (act_n, down_w))[a]
        term = jnp.dot(source[...], weight[at], preferred_element_type=jnp.float32)
        parts[a, at] = term.astype(jnp.bfloat16).reshape(parts.shape[2:])
        if a == 0:
            rows = rows_all[1, at].reshape(tokens, quarter).astype(jnp.float32)
            g = gains_s[:, pl.ds(pl.multiple_of(at * quarter, quarter), quarter)]
            own = jnp.where(modality == 0.0, g[0:1, :], jnp.where(modality == 1.0, g[1:2, :], g[2:3, :]))
            total = jnp.sum(term * rows, axis=0, keepdims=True) / own
            chunk = width // dp
            for j in range(quarter // chunk):
                for r in range(8):
                    first = j * chunk + r * HD
                    gain_mine[at * (quarter // chunk) + j, r : r + 1, :] = total[:, first : first + HD]

    def add(dst, src):
        dst[...] = (dst[...].astype(jnp.float32) + src[...].astype(jnp.float32)).astype(jnp.bfloat16)

    ways = list(range(1, lines)) + [0]

    def core_near(a):
        other = (1 - y) * 2
        partial_sum(a, other + 1 - c)
        to_core(a, 1).start()
        partial_sum(a, other + c)

    def core_far(a):
        other = (1 - y) * 2
        partial_sum(a, y * 2 + 1 - c)
        to_core(a, 0).start()
        to_core(a, 1).wait_recv()
        add(parts.at[a, other + c], from_core.at[a, 1])
        for k in ways:
            to_second(a, 1, k).start()
        partial_sum(a, s)
        to_core(a, 0).wait_recv()
        add(parts.at[a, s], from_core.at[a, 0])
        for k in ways:
            to_second(a, 0, k).start()

    def second_sums(a):
        gy, gi, _ = side(a, 1, 0)
        for k in ways:
            to_second(a, 1, k).wait_recv()
            add(parts.at[a, gy * 2 + c, gi, flip(line, k)], from_second.at[a, 1, k])
            to_first(a, k).start()

    def side_sum(a, k):
        to_second(a, 0, k).wait_recv()
        to_first(a, k).wait_recv()
        return (
            parts[a, s, inner, flip(line, k)].astype(jnp.float32)
            + from_second[a, 0, k].astype(jnp.float32)
            + from_first[a, k].astype(jnp.float32)
        )

    def first_sums(a):
        for k in range(1, lines):
            parts[a, s, inner, flip(line, k)] = side_sum(a, k).astype(jnp.bfloat16)
            to_line(a, k).start()

    def line_sums(a):
        total = side_sum(a, 0)
        for k in range(1, lines):
            to_line(a, k).wait_recv()
            total = total + from_line[a, k].astype(jnp.float32)
        return total

    def gain_scatter(k):
        target = flip(d, k)
        return send(gain_mine.at[target], gain_inbox.at[k], gs_send.at[k], gs_recv.at[k], (target, s))

    def gain_spread(k):
        return send(gain_own, gain_ref.at[s, d], gd_send.at[k], gd_recv.at[k], (flip(d, k), s))

    def gain_across(k):
        return send(gain_ref.at[s], gain_ref.at[s], gx_send.at[k], gx_recv.at[k], (d, flip(s, k)))

    own = LENGTH // slots
    part = quarter // slots

    def pack(a, block):
        row = lax.broadcasted_iota(jnp.int32, (slots * LENGTH, LENGTH), 0)
        token = lax.broadcasted_iota(jnp.int32, (slots * LENGTH, LENGTH), 1)
        wanted = (row // LENGTH) * own + row % own
        place = (row % LENGTH) // own
        total = jnp.zeros((slots * LENGTH, part), jnp.float32)
        for j in range(slots):
            pick = ((place == j) & (token == wanted)).astype(jnp.bfloat16)
            total = total + jnp.dot(pick, block[:, j * part : (j + 1) * part], preferred_element_type=jnp.float32)
        packed[a] = total.astype(jnp.bfloat16).reshape(slots, LENGTH, part)
        sums_ref[a, s] = packed[a, s]

    def spread(a, k):
        target = flip(s, k)
        return send(packed.at[a, target], sums_ref.at[a, s], spread_send.at[a, k], spread_recv.at[a, k], (d, target))

    core_near(0)
    core_far(0)
    for k in range(1, dp):
        gain_scatter(k).start()
    preact = pre_t[...]
    activated = jnp.where(keep, preact * jax.nn.sigmoid(preact), 0.0)
    act_t[...] = activated.astype(jnp.bfloat16)
    keep_act.start()
    act_n[...] = activated.T.astype(jnp.bfloat16)
    core_near(1)
    second_sums(0)
    core_far(1)
    first_sums(0)
    second_sums(1)
    gain_total = gain_mine[d]
    for k in range(1, dp):
        gain_scatter(k).wait_recv()
        gain_total = gain_total + gain_inbox[k]
    gain_own[...] = gain_total
    gain_ref[s, d] = gain_total
    for k in range(1, dp):
        gain_spread(k).start()
    norm_grad = line_sums(0)
    hid_f = hidden_s[...].astype(jnp.float32)
    normed_f = hid_f * inverse
    scaled = norm_grad * gain_rows()
    own_stat = jnp.sum(scaled * normed_f, axis=-1, keepdims=True)
    stat[1, 0] = jnp.broadcast_to(own_stat, (LENGTH, HD))
    for k in range(1, slots):
        send_stat(1, k).start()
    first_sums(1)
    for k in range(1, dp):
        gain_spread(k).wait_recv()
    for k in range(1, slots):
        gain_across(k).start()
    for k in range(1, slots):
        send_stat(1, k).wait_recv()
    mean = (stat[1, 0] + stat[1, 1] + stat[1, 2] + stat[1, 3])[:, :1] / width
    cot_f = rows_all[0, s, inner, line].astype(jnp.float32)
    res_grad = (cot_f + inverse * (scaled - normed_f * mean)).astype(jnp.bfloat16)
    pack(0, res_grad)
    for k in range(1, slots):
        spread(0, k).start()
    pack(1, (hidden_s[...].astype(jnp.float32) + line_sums(1)).astype(jnp.bfloat16))
    for k in range(1, slots):
        spread(1, k).start()
    query, key, value = (stack_heads(ref[...]) for ref in (query_s, key_s, value_s))
    grad = stack_heads(res_grad)
    probs = probs_s[...]
    value_grad = contract_first(probs_b_s[...], grad)
    dprob = contract_last(grad, value)
    delta = jnp.sum(grad.astype(jnp.float32) * attended_s[...].astype(jnp.float32), axis=-1, keepdims=True)
    dscore = (probs * (dprob - delta) * HD ** (-0.5)).astype(jnp.bfloat16)
    query_grad = jnp.dot(dscore, key, preferred_element_type=jnp.float32)
    key_grad = contract_first(dscore, query)
    for place, heads in ((0, query_grad), (1, key_grad), (2, value_grad)):
        for h in range(quarter // HD):
            heads_ref[place, :, h * HD : (h + 1) * HD] = heads[h * LENGTH : (h + 1) * LENGTH, :].astype(jnp.bfloat16)
    keep_rows.wait()
    keep_act.wait()
    keep_pre_grad.wait()
    for a in range(2):
        gather_end(a)
        for k in range(1, slots):
            send_stat(a, k).wait_send()
        for f in range(2):
            to_core(a, f).wait_send()
            for k in range(lines):
                to_second(a, f, k).wait_send()
        for k in range(lines):
            to_first(a, k).wait_send()
        for k in range(1, lines):
            to_line(a, k).wait_send()
    for k in range(1, dp):
        send_tag(k).wait_send()
        gain_scatter(k).wait_send()
        gain_spread(k).wait_send()
    for k in range(1, slots):
        gain_across(k).wait_recv()
        gain_across(k).wait_send()
    for a in range(2):
        for k in range(1, slots):
            spread(a, k).wait_recv()
            spread(a, k).wait_send()


LENGTH = 16


def layer(dp, slots, labels, slot_modality, queries, keys, values, residual, gains, up_weight, down_weight, cotangent):
    lines = dp // 2
    quarter = queries.shape[2]
    hidden_units = up_weight.shape[1]
    tokens = dp * LENGTH
    width = quarter * slots
    bf, f32 = jnp.bfloat16, jnp.float32
    any_space = pl.BlockSpec(memory_space=pl.ANY)
    scalar = pl.BlockSpec(memory_space=pltpu.SMEM)
    vm = pl.BlockSpec(memory_space=pltpu.VMEM)
    dma = pltpu.SemaphoreType.DMA
    rows_shape = (2, slots, 2, lines, LENGTH, quarter)
    chunk = width // dp
    return pl.pallas_call(
        functools.partial(layer_kernel, (lines, dp, slots, quarter, hidden_units)),
        out_shape=(
            jax.ShapeDtypeStruct((hidden_units, tokens), bf),
            jax.ShapeDtypeStruct((hidden_units, tokens), bf),
            jax.ShapeDtypeStruct(rows_shape, bf),
            jax.ShapeDtypeStruct((2, slots, LENGTH, quarter // slots), bf),
            jax.ShapeDtypeStruct((slots, dp, 8, chunk // 8), f32),
            jax.ShapeDtypeStruct((3, LENGTH, quarter), bf),
        ),
        in_specs=[scalar, scalar] + [any_space] * 8,
        out_specs=(any_space, any_space, any_space, vm, vm, vm),
        scratch_shapes=[
            pltpu.VMEM((slots, hidden_units, quarter), bf),
            pltpu.VMEM((slots, hidden_units, quarter), bf),
            pltpu.VMEM(rows_shape, bf),
            pltpu.VMEM((LENGTH, quarter), bf),
            pltpu.VMEM((LENGTH, quarter), bf),
            pltpu.VMEM((LENGTH, quarter), bf),
            pltpu.VMEM((LENGTH, quarter), bf),
            pltpu.VMEM(gains.shape, f32),
            pltpu.VMEM((LENGTH, quarter), bf),
            pltpu.VMEM((quarter // HD * LENGTH, HD), bf),
            pltpu.VMEM((quarter // HD * LENGTH, quarter // HD * LENGTH), f32),
            pltpu.VMEM((quarter // HD * LENGTH, quarter // HD * LENGTH), bf),
            pltpu.VMEM((2, slots, LENGTH, quarter // slots), bf),
            pltpu.VMEM((2, slots, LENGTH, HD), f32),
            pltpu.VMEM((dp, 8, tokens), f32),
            pltpu.VMEM((hidden_units, tokens), f32),
            pltpu.VMEM((hidden_units, tokens), f32),
            pltpu.VMEM((hidden_units, tokens), bf),
            pltpu.VMEM((hidden_units, tokens), bf),
            pltpu.VMEM((tokens, hidden_units), bf),
            pltpu.VMEM((tokens, hidden_units), bf),
            pltpu.VMEM(rows_shape, bf),
            pltpu.VMEM((2, 2, 2, lines, LENGTH, quarter), bf),
            pltpu.VMEM((2, 2, lines, LENGTH, quarter), bf),
            pltpu.VMEM((2, lines, LENGTH, quarter), bf),
            pltpu.VMEM((2, lines, LENGTH, quarter), bf),
            pltpu.VMEM((dp, 8, chunk // 8), f32),
            pltpu.VMEM((dp, 8, chunk // 8), f32),
            pltpu.VMEM((8, chunk // 8), f32),
            dma((6,)), dma((2, slots)),
            dma((dp,)), dma((dp,)),
            dma((2, slots)), dma((2, slots)),
            dma((2, lines)), dma((2, lines)),
            dma((2, lines)), dma((2, lines)),
            dma((2, 2, lines)), dma((2, 2, lines)),
            dma((2, 4)), dma((2, 4)),
            dma((2, 2)), dma((2, 2)),
            dma((2, 2, lines)), dma((2, 2, lines)),
            dma((2, lines)), dma((2, lines)),
            dma((2, lines)), dma((2, lines)),
            dma((2, slots)), dma((2, slots)),
            dma((dp,)), dma((dp,)),
            dma((dp,)), dma((dp,)),
            dma((slots,)), dma((slots,)),
            dma((3,)),
        ],
        compiler_params=pltpu.CompilerParams(
            collective_id=0, has_side_effects=True, vmem_limit_bytes=62 * 1024 * 1024
        ),
    )(labels, slot_modality, queries, keys, values, residual, gains, up_weight, down_weight, cotangent)


def grads_kernel(
    modality_ref, act_ref, pre_grad_ref, rows_ref, cots_ref, sums_ref, gain_ref, heads_ref,
    out_ref, res_grad_ref, query_grad_ref, key_grad_ref, value_grad_ref, up_grad_ref, down_grad_ref, gain_grad_ref,
):
    step = pl.program_id(0)
    rows = rows_ref[0, 0].reshape(-1, rows_ref.shape[-1])
    cots = cots_ref[0, 0].reshape(-1, cots_ref.shape[-1])
    up_grad_ref[...] = jnp.dot(pre_grad_ref[...], rows, preferred_element_type=jnp.float32).astype(jnp.bfloat16)
    down_grad_ref[...] = jnp.dot(act_ref[...], cots, preferred_element_type=jnp.float32).astype(jnp.bfloat16)

    @pl.when(step == 1)
    def _():
        for place, ref in enumerate((query_grad_ref, key_grad_ref, value_grad_ref)):
            ref[0] = heads_ref[place]
        slots, part = sums_ref.shape[1], sums_ref.shape[3]
        own = LENGTH // slots
        for a, ref in ((0, res_grad_ref), (1, out_ref)):
            for q in range(slots):
                packed = sums_ref[a, q].astype(jnp.float32)
                for j in range(slots):
                    first = (q * slots + j) * part
                    ref[0, :, first : first + part] = packed[j * own : (j + 1) * own, :].astype(jnp.bfloat16)

    @pl.when(step == 2)
    def _():
        slots, dp, lanes = gain_ref.shape[0], gain_ref.shape[1], gain_ref.shape[3]
        for m in range(gain_grad_ref.shape[0]):
            total = jnp.zeros(gain_ref.shape[1:], jnp.float32)
            for q in range(slots):
                total = total + jnp.where(modality_ref[q] == m, gain_ref[q], 0.0)
            for j in range(dp):
                for r in range(8):
                    first = (j * 8 + r) * lanes
                    gain_grad_ref[m : m + 1, first : first + lanes] = total[j, r : r + 1, :]


def grads(act, pre_grad, rows, sums, gain, heads, slot_modality, width):
    hidden_units, tokens = act.shape
    _, slots, inner, lines, length, quarter = rows.shape
    bf, f32 = jnp.bfloat16, jnp.float32
    halves = 2
    columns = quarter // halves
    scalar = pl.BlockSpec(memory_space=pltpu.SMEM)

    def whole(shape):
        return pl.BlockSpec(shape, lambda i: (0,) * len(shape))

    def block(a):
        return pl.BlockSpec(
            (1, 1, inner, lines, length, columns), lambda i: (a, i // halves, 0, 0, 0, i % halves)
        )

    own = (1, length // slots, width)
    head = (1, length, quarter)
    weight = pl.BlockSpec((hidden_units, columns), lambda i: (0, i))
    return pl.pallas_call(
        grads_kernel,
        grid=(slots * halves,),
        out_shape=(
            jax.ShapeDtypeStruct(own, bf),
            jax.ShapeDtypeStruct(own, bf),
            jax.ShapeDtypeStruct(head, bf),
            jax.ShapeDtypeStruct(head, bf),
            jax.ShapeDtypeStruct(head, bf),
            jax.ShapeDtypeStruct((hidden_units, width), bf),
            jax.ShapeDtypeStruct((hidden_units, width), bf),
            jax.ShapeDtypeStruct((MODALITIES, width), f32),
        ),
        in_specs=[
            scalar, whole(act.shape), whole(act.shape), block(1), block(0), whole(sums.shape), whole(gain.shape),
            whole(heads.shape),
        ],
        out_specs=(
            whole(own), whole(own), whole(head), whole(head), whole(head), weight, weight, whole((MODALITIES, width)),
        ),
        compiler_params=pltpu.CompilerParams(
            dimension_semantics=("arbitrary",), vmem_limit_bytes=VMEM_BYTES
        ),
    )(slot_modality, act, pre_grad, rows, rows, sums, gain, heads)


def fast_on_device(
    dp, slots, queries, keys, values, residual, labels, slot_modality, gains, up_weight, down_weight, cotangent
):
    act, pre_grad, rows, sums, gain, heads = layer(
        dp, slots, labels, slot_modality, queries, keys, values, residual, gains, up_weight, down_weight, cotangent
    )
    output, residual_grad, query_grad, key_grad, value_grad, up_grad, down_grad, gain_grad = grads(
        act, pre_grad, rows, sums, gain, heads, slot_modality, residual.shape[2]
    )
    return (
        output, residual_grad, query_grad, key_grad, value_grad, up_grad[None], down_grad[None], gain_grad,
    )


def solution(mesh):
    in_specs = (
        P("dp", None, "sect"),
        P("dp", None, "sect"),
        P("dp", None, "sect"),
        P("dp", None, None),
        P("dp", None),
        P(),
        P(),
        P("sect", "dp", None),
        P("sect", "dp", None),
        P("dp", None, None),
    )
    out_specs = (
        P("dp", "sect", None),
        P("dp", "sect", None),
        P("dp", None, "sect"),
        P("dp", None, "sect"),
        P("dp", None, "sect"),
        P("sect", "dp", None),
        P("sect", "dp", None),
        P(),
    )
    dp, slots = mesh.shape["dp"], mesh.shape["sect"]
    body = functools.partial(fast_on_device if (dp, slots) == (8, 4) else on_device, dp, slots)
    return jax.shard_map(
        body, mesh=mesh, in_specs=in_specs, out_specs=out_specs, check_vma=False
    )
```

```python
import functools

import jax
import jax.numpy as jnp
from jax import lax
from jax.experimental import pallas as pl
from jax.experimental.pallas import tpu as pltpu
from jax.sharding import PartitionSpec as P

HD = 128
MODALITIES = 3


def causal_forward(queries, keys, values):
    seq_count, length, width = queries.shape
    head_count = width // HD
    query_f = queries.astype(jnp.float32).reshape(seq_count, length, head_count, HD)
    key_f = keys.astype(jnp.float32).reshape(seq_count, length, head_count, HD)
    value_f = values.astype(jnp.float32).reshape(seq_count, length, head_count, HD)
    scores = jnp.einsum("sqhd,skhd->shqk", query_f, key_f) * HD ** (-0.5)
    position = jnp.arange(length)
    causal = position[:, None] >= position[None, :]
    scores = jnp.where(causal, scores, -1e30)
    probs = jax.nn.softmax(scores, axis=-1)
    probs_b = probs.astype(jnp.bfloat16)
    attended = jnp.einsum("shqk,skhd->sqhd", probs_b.astype(jnp.float32), value_f)
    return (attended.astype(jnp.bfloat16).reshape(seq_count, length, width), probs, probs_b)


def causal_backward(grad_out, queries, keys, values, attended, probs, probs_b):
    seq_count, length, width = queries.shape
    head_count = width // HD
    shape = (seq_count, length, head_count, HD)
    grad_f = grad_out.astype(jnp.float32).reshape(shape)
    query_f = queries.astype(jnp.float32).reshape(shape)
    key_f = keys.astype(jnp.float32).reshape(shape)
    value_f = values.astype(jnp.float32).reshape(shape)
    attended_f = attended.astype(jnp.float32).reshape(shape)
    value_grad = jnp.einsum("shqk,sqhd->skhd", probs_b.astype(jnp.float32), grad_f).astype(
        jnp.bfloat16
    )
    dprob = jnp.einsum("sqhd,skhd->shqk", grad_f, value_f)
    delta = jnp.einsum("sqhd,sqhd->shq", grad_f, attended_f)
    dscore = (
        (probs * (dprob - delta[..., None]) * HD ** (-0.5)).astype(jnp.bfloat16).astype(jnp.float32)
    )
    query_grad = jnp.einsum("shqk,skhd->sqhd", dscore, key_f).astype(jnp.bfloat16)
    key_grad = jnp.einsum("shqk,sqhd->skhd", dscore, query_f).astype(jnp.bfloat16)
    return (
        query_grad.reshape(seq_count, length, width),
        key_grad.reshape(seq_count, length, width),
        value_grad.reshape(seq_count, length, width),
    )


MESH = pl.DeviceIdType.MESH
VMEM_BYTES = 60 * 1024 * 1024


def remote(src, dst, send_sem, recv_sem, dp_index, sect_index):
    return pltpu.make_async_remote_copy(
        src_ref=src,
        dst_ref=dst,
        send_sem=send_sem,
        recv_sem=recv_sem,
        device_id=(dp_index, sect_index),
        device_id_type=MESH,
    )


def greet(peers):
    barrier = pltpu.get_barrier_semaphore()
    total = jnp.int32(0)
    for dp_index, sect_index, present in peers:
        if present is None:
            pl.semaphore_signal(barrier, inc=1, device_id=(dp_index, sect_index), device_id_type=MESH)
            total = total + 1
        else:

            @pl.when(present)
            def _():
                pl.semaphore_signal(
                    barrier, inc=1, device_id=(dp_index, sect_index), device_id_type=MESH
                )

            total = total + present.astype(jnp.int32)
    pl.semaphore_wait(barrier, total)


class LineGather:
    def __init__(self, buf, sems, lines, slot):
        self.buf, self.lines = buf, lines
        self.send_sems, self.recv_sems = sems
        self.slot = slot
        self.me = lax.axis_index("dp")
        self.sect = lax.axis_index("sect")
        self.outer, self.inner = self.me // 2, self.me % 2

    def copy(self, way, outer, target, incoming=False):
        inner = (1 - self.inner) if (incoming and way == 2) else self.inner
        block = self.buf.at[outer * 2 + inner]
        recv = 1 if way == 2 else 0
        return remote(
            block,
            block,
            self.send_sems.at[self.slot, way, outer],
            self.recv_sems.at[self.slot, recv, outer],
            target,
            self.sect,
        )

    def pass_up(self, outer):
        return self.copy(0, outer, jnp.minimum(self.outer + 1, self.lines - 1) * 2 + self.inner)

    def pass_down(self, outer):
        return self.copy(1, outer, jnp.maximum(self.outer - 1, 0) * 2 + self.inner)

    def pass_across(self, outer):
        return self.copy(2, outer, self.outer * 2 + 1 - self.inner)

    def start(self):
        outer = self.outer

        @pl.when(outer + 1 < self.lines)
        def _():
            self.pass_up(outer).start()

        @pl.when(outer > 0)
        def _():
            self.pass_down(outer).start()

        self.pass_across(outer).start()

    def relay(self, step):
        outer = self.outer

        @pl.when(outer - step >= 0)
        def _():
            block = outer - step
            self.pass_down(block).wait_recv()

            @pl.when(outer + 1 < self.lines)
            def _():
                self.pass_up(block).start()

            self.pass_across(block).start()

        @pl.when(outer + step < self.lines)
        def _():
            block = outer + step
            self.pass_up(block).wait_recv()

            @pl.when(outer > 0)
            def _():
                self.pass_down(block).start()

            self.pass_across(block).start()

    def finish(self):
        outer = self.outer
        for block in range(self.lines):
            self.copy(2, block, self.outer * 2 + 1 - self.inner, incoming=True).wait_recv()
            self.pass_across(block).wait_send()

            @pl.when((outer + 1 < self.lines) & (block <= outer))
            def _():
                self.pass_up(block).wait_send()

            @pl.when((outer > 0) & (block >= outer))
            def _():
                self.pass_down(block).wait_send()


def front_kernel(
    lines, slots, att_ref, res_ref, gain_ref, sel_ref, cot_ref, hidden_ref, norm_ref, rows_ref, cots_ref,
    att_all, send_sems, recv_sems, att_send, att_recv,
):
    me, sect = lax.axis_index("dp"), lax.axis_index("sect")
    outer, inner = me // 2, me % 2
    width = att_ref.shape[1]
    peers = [(me, lax.rem(sect + k, slots), None) for k in range(1, slots)]
    peers.append((outer * 2 + 1 - inner, sect, None))
    peers.append((jnp.minimum(outer + 1, lines - 1) * 2 + inner, sect, outer + 1 < lines))
    peers.append((jnp.maximum(outer - 1, 0) * 2 + inner, sect, outer > 0))
    sel = sel_ref[...]
    cots_ref[me] = jnp.dot(sel, cot_ref[...], preferred_element_type=jnp.float32).astype(jnp.bfloat16)
    greet(peers)
    copies = []
    for k in range(1, slots):
        target = lax.rem(sect + k, slots)
        copies.append(
            remote(att_ref, att_all.at[sect], att_send.at[k], att_recv.at[sect], me, target)
        )
        copies[-1].start()
    cots = LineGather(cots_ref, (send_sems, recv_sems), lines, 0)
    rows = LineGather(rows_ref, (send_sems, recv_sems), lines, 1)
    cots.start()
    att_all[sect] = att_ref[...]
    for k in range(1, slots):
        source = lax.rem(sect + k, slots)
        remote(att_ref, att_all.at[source], att_send.at[k], att_recv.at[source], me, source).wait_recv()
    square = jnp.zeros((res_ref.shape[0], 1), jnp.float32)
    for block in range(slots):
        cols = slice(block * width, (block + 1) * width)
        hid = (
            res_ref[:, cols].astype(jnp.float32) + att_all[block].astype(jnp.float32)
        ).astype(jnp.bfloat16)
        hidden_ref[:, cols] = hid
        hid_f = hid.astype(jnp.float32)
        square = square + jnp.sum(hid_f * hid_f, axis=-1, keepdims=True)
    inverse = lax.rsqrt(square / (slots * width) + 1e-05)
    norm_ref[...] = jnp.broadcast_to(inverse, norm_ref.shape)
    for block in range(slots):
        cols = slice(block * width, (block + 1) * width)
        normed = (hidden_ref[:, cols].astype(jnp.float32) * inverse * gain_ref[:, cols]).astype(
            jnp.bfloat16
        )
        rows_ref[me, :, cols] = jnp.dot(sel, normed, preferred_element_type=jnp.float32).astype(
            jnp.bfloat16
        )
    rows.start()
    for step in range(1, lines):
        cots.relay(step)
        rows.relay(step)
    cots.finish()
    rows.finish()
    for one in copies:
        one.wait_send()


def front(att, residual, gain_rows, selector, cotangent, dp, slots):
    length, width = residual.shape
    capacity = selector.shape[0]
    vm = pl.BlockSpec(memory_space=pltpu.VMEM)
    return pl.pallas_call(
        functools.partial(front_kernel, dp // 2, slots),
        out_shape=(
            jax.ShapeDtypeStruct((length, width), jnp.bfloat16),
            jax.ShapeDtypeStruct((length, 128), jnp.float32),
            jax.ShapeDtypeStruct((dp, capacity, width), jnp.bfloat16),
            jax.ShapeDtypeStruct((dp, capacity, width), jnp.bfloat16),
        ),
        in_specs=[vm] * 5,
        out_specs=(vm,) * 4,
        scratch_shapes=[
            pltpu.VMEM((slots,) + att.shape, jnp.bfloat16),
            pltpu.SemaphoreType.DMA((2, 3, dp // 2)),
            pltpu.SemaphoreType.DMA((2, 2, dp // 2)),
            pltpu.SemaphoreType.DMA((slots,)),
            pltpu.SemaphoreType.DMA((slots,)),
        ],
        compiler_params=pltpu.CompilerParams(
            collective_id=0, has_side_effects=True, vmem_limit_bytes=VMEM_BYTES
        ),
    )(att, residual, gain_rows, selector, cotangent)


def ffn_kernel(tail, rows_ref, cots_ref, up_ref, down_ref, out_ref, back_ref, upg_ref, downg_ref, out_acc, back_acc):
    step = pl.program_id(0)
    last = pl.num_programs(0) - 1
    full = up_ref.shape[0]

    @pl.when(step == 0)
    def _():
        out_acc[...] = jnp.zeros_like(out_acc)
        back_acc[...] = jnp.zeros_like(back_acc)

    def run(size):
        rows, cots = rows_ref[...], cots_ref[...]
        preact = contract_last(rows, up_ref[:size, :])
        back = contract_last(cots, down_ref[:size, :])
        sigma = jax.nn.sigmoid(preact)
        activated = (preact * sigma).astype(jnp.bfloat16)
        pre_grad = (back * sigma * (1.0 + preact * (1.0 - sigma))).astype(jnp.bfloat16)
        out_acc[...] += jnp.dot(activated, down_ref[:size, :], preferred_element_type=jnp.float32)
        back_acc[...] += jnp.dot(pre_grad, up_ref[:size, :], preferred_element_type=jnp.float32)
        downg_ref[:size, :] = contract_first(activated, cots).astype(jnp.bfloat16)
        upg_ref[:size, :] = contract_first(pre_grad, rows).astype(jnp.bfloat16)

    if tail == full:
        run(full)
    else:

        @pl.when(step < last)
        def _():
            run(full)

        @pl.when(step == last)
        def _():
            run(tail)

    @pl.when(step == last)
    def _():
        out_ref[...] = out_acc[...].astype(jnp.bfloat16)
        back_ref[...] = back_acc[...].astype(jnp.bfloat16)


def ffn(rows, cots, up, down):
    count, width = rows.shape
    hidden_units = up.shape[0]
    chunk = min(256 if count <= 128 else 128, hidden_units)
    steps = pl.cdiv(hidden_units, chunk)
    tail = hidden_units - (steps - 1) * chunk
    whole = pl.BlockSpec((count, width), lambda i: (0, 0))
    weight = pl.BlockSpec((chunk, width), lambda i: (i, 0))
    return pl.pallas_call(
        functools.partial(ffn_kernel, tail),
        grid=(steps,),
        out_shape=(
            jax.ShapeDtypeStruct((count, width), jnp.bfloat16),
            jax.ShapeDtypeStruct((count, width), jnp.bfloat16),
            jax.ShapeDtypeStruct(up.shape, jnp.bfloat16),
            jax.ShapeDtypeStruct(down.shape, jnp.bfloat16),
        ),
        in_specs=[whole, whole, weight, weight],
        out_specs=(whole, whole, weight, weight),
        scratch_shapes=[
            pltpu.VMEM((count, width), jnp.float32),
            pltpu.VMEM((count, width), jnp.float32),
        ],
        compiler_params=pltpu.CompilerParams(
            dimension_semantics=("arbitrary",), vmem_limit_bytes=VMEM_BYTES
        ),
    )(rows, cots, up, down)


def reduce_kernel(lines, slots, out_in, back_in, sums_ref, from_pair, pair_sum, from_line, pair_send, pair_recv,
                  line_send, line_recv, sect_send, sect_recv):
    me, sect = lax.axis_index("dp"), lax.axis_index("sect")
    outer, inner = me // 2, me % 2
    partner = outer * 2 + 1 - inner
    terms = (back_in, out_in)
    peers = [(me, lax.rem(sect + k, slots), None) for k in range(1, slots)]
    peers.append((partner, sect, None))
    for k in range(1, lines):
        peers.append((lax.rem(outer + k, lines) * 2 + inner, sect, None))
    greet(peers)
    order = [(k, step) for k in range(2) for step in list(range(1, lines)) + [0]]

    def across(k, step):
        line = lax.rem(outer + step, lines)
        return remote(
            terms[k].at[line * 2 + 1 - inner],
            from_pair.at[k, step],
            pair_send.at[k, step],
            pair_recv.at[k, step],
            partner,
            sect,
        )

    def along(k, step):
        line = lax.rem(outer + step, lines)
        return remote(
            pair_sum.at[k, step],
            from_line.at[k, step],
            line_send.at[k, step],
            line_recv.at[k, step],
            line * 2 + inner,
            sect,
        )

    def to_sect(k, hop):
        target = lax.rem(sect + hop, slots)
        return remote(
            sums_ref.at[k, sect],
            sums_ref.at[k, sect],
            sect_send.at[k, hop],
            sect_recv.at[k, sect],
            me,
            target,
        )

    def from_sect(k, hop):
        source = lax.rem(sect + hop, slots)
        return remote(
            sums_ref.at[k, source],
            sums_ref.at[k, source],
            sect_send.at[k, hop],
            sect_recv.at[k, source],
            me,
            source,
        )

    for k, step in order:
        across(k, step).start()
    for k in range(2):
        for step in list(range(1, lines)) + [0]:
            across(k, step).wait_recv()
            line = lax.rem(outer + step, lines)
            own = terms[k][line * 2 + inner].astype(jnp.float32) + from_pair[k, step].astype(jnp.float32)
            if step:
                pair_sum[k, step] = own.astype(jnp.bfloat16)
                along(k, step).start()
        for step in range(1, lines):
            along(k, step).wait_recv()
            own = own + from_line[k, step].astype(jnp.float32)
        sums_ref[k, sect] = own.astype(jnp.bfloat16)
        for hop in range(1, slots):
            to_sect(k, hop).start()
    for k in range(2):
        for hop in range(1, slots):
            from_sect(k, hop).wait_recv()
            to_sect(k, hop).wait_send()
        for step in range(lines):
            across(k, step).wait_send()
            if step:
                along(k, step).wait_send()


def reduce_terms(out_terms, back_terms, slots):
    dp, capacity, width = out_terms.shape
    lines = dp // 2
    vm = pl.BlockSpec(memory_space=pltpu.VMEM)
    dma = pltpu.SemaphoreType.DMA
    return pl.pallas_call(
        functools.partial(reduce_kernel, lines, slots),
        out_shape=jax.ShapeDtypeStruct((2, slots, capacity, width), jnp.bfloat16),
        in_specs=[vm] * 2,
        out_specs=vm,
        scratch_shapes=[
            pltpu.VMEM((2, lines, capacity, width), jnp.bfloat16),
            pltpu.VMEM((2, lines, capacity, width), jnp.bfloat16),
            pltpu.VMEM((2, lines, capacity, width), jnp.bfloat16),
            dma((2, lines)),
            dma((2, lines)),
            dma((2, lines)),
            dma((2, lines)),
            dma((2, slots)),
            dma((2, slots)),
        ],
        compiler_params=pltpu.CompilerParams(
            collective_id=1, has_side_effects=True, vmem_limit_bytes=VMEM_BYTES
        ),
    )(out_terms, back_terms)


def gain_kernel(dp, slots, part_ref, total_ref, inbox, mine, first_send, first_recv, next_send, next_recv, sect_send, sect_recv):
    me, sect = lax.axis_index("dp"), lax.axis_index("sect")
    peers = [(me, lax.rem(sect + k, slots), None) for k in range(1, slots)]
    peers += [(lax.rem(me + k, dp), sect, None) for k in range(1, dp)]
    greet(peers)

    def scatter(k):
        target = lax.rem(me + k, dp)
        return remote(
            part_ref.at[sect, target], inbox.at[k], first_send.at[k], first_recv.at[k], target, sect
        )

    def spread_sum(k):
        target = lax.rem(me + k, dp)
        return remote(
            mine, total_ref.at[sect, me], next_send.at[k], next_recv.at[k], target, sect
        )

    def to_sect(k):
        return remote(
            total_ref.at[sect],
            total_ref.at[sect],
            sect_send.at[k],
            sect_recv.at[k],
            me,
            lax.rem(sect + k, slots),
        )

    for k in range(1, dp):
        scatter(k).start()
    total = part_ref[sect, me]
    for k in range(1, dp):
        scatter(k).wait_recv()
        total = total + inbox[k]
    mine[...] = total
    for k in range(1, dp):
        spread_sum(k).start()
    total_ref[sect, me] = total
    for k in range(1, dp):
        spread_sum(k).wait_recv()
    for k in range(1, slots):
        to_sect(k).start()
    for k in range(1, slots):
        to_sect(k).wait_recv()
        to_sect(k).wait_send()
    for k in range(1, dp):
        scatter(k).wait_send()
        spread_sum(k).wait_send()


def gain_sum(part, dp, slots):
    kinds, width = part.shape
    cols = width // (dp * slots)
    padded = jnp.concatenate([part, jnp.zeros((8 - kinds, width), part.dtype)], 0)
    pieces = padded.reshape(8, slots, dp, cols).transpose(1, 2, 0, 3)
    vm = pl.BlockSpec(memory_space=pltpu.VMEM)
    dma = pltpu.SemaphoreType.DMA
    total = pl.pallas_call(
        functools.partial(gain_kernel, dp, slots),
        out_shape=jax.ShapeDtypeStruct(pieces.shape, pieces.dtype),
        in_specs=[vm],
        out_specs=vm,
        scratch_shapes=[
            pltpu.VMEM((dp, 8, cols), pieces.dtype),
            pltpu.VMEM((8, cols), pieces.dtype),
            dma((dp,)),
            dma((dp,)),
            dma((dp,)),
            dma((dp,)),
            dma((slots,)),
            dma((slots,)),
        ],
        compiler_params=pltpu.CompilerParams(collective_id=2, has_side_effects=True),
    )(pieces)
    return total.transpose(2, 0, 1, 3).reshape(8, width)[:kinds]


def contract_last(left, right):
    return lax.dot_general(
        left, right, (((1,), (1,)), ((), ())), preferred_element_type=jnp.float32
    )


def contract_first(left, right):
    return lax.dot_general(
        left, right, (((0,), (0,)), ((), ())), preferred_element_type=jnp.float32
    )


def selectors(token_labels, slot_modality):
    length = token_labels.shape[0]
    keep = token_labels[None, :] == slot_modality[:, None]
    upto = jnp.arange(length)[None, :] <= jnp.arange(length)[:, None]
    rank = jnp.sum((keep[:, None, :] & upto[None]).astype(jnp.int32), axis=2) - 1
    capacity = length // 2
    return (rank[:, None, :] == jnp.arange(capacity)[None, :, None]) & keep[:, None, :]


def on_device(
    dp, slots, queries, keys, values, residual, labels, slot_modality, gains, up_weight, down_weight, cotangent
):
    attended_block, probs, probs_b = causal_forward(queries, keys, values)
    token_labels = labels[0]
    onehot = (token_labels[:, None] == jnp.arange(MODALITIES)[None, :]).astype(jnp.float32)
    gain_rows = jnp.dot(onehot, gains, precision=lax.Precision.HIGHEST)
    slot_index = lax.axis_index("sect")
    all_select = selectors(token_labels, slot_modality).astype(jnp.bfloat16)
    selector = lax.dynamic_index_in_dim(all_select, slot_index, 0, keepdims=False)
    capacity, length = selector.shape
    grad_full = cotangent[0]
    hidden, inverse, rows, cots = front(
        attended_block[0], residual[0], gain_rows, selector, grad_full, dp, slots
    )
    width = hidden.shape[1]
    inverse = inverse[:, :1]
    hidden_f = hidden.astype(jnp.float32)
    normed_f = hidden_f * inverse
    out_terms, back_terms, up_grad, down_grad = ffn(
        rows.reshape(-1, width), cots.reshape(-1, width), up_weight[0], down_weight[0]
    )
    sums = reduce_terms(
        out_terms.reshape(dp, capacity, width), back_terms.reshape(dp, capacity, width), slots
    ).reshape(2, slots * capacity, width)
    place = all_select.reshape(slots * capacity, length)
    norm_grad = contract_first(place, sums[0])
    quarter = length // slots
    place_own = lax.dynamic_slice_in_dim(place, slot_index * quarter, quarter, 1)
    hidden_own = lax.dynamic_slice_in_dim(hidden_f, slot_index * quarter, quarter, 0)
    output = (hidden_own + contract_first(place_own, sums[1])).astype(jnp.bfloat16)[None]
    scaled = norm_grad * gain_rows
    hidden_grad = grad_full.astype(jnp.float32) + inverse * (
        scaled - normed_f * jnp.mean(scaled * normed_f, axis=-1, keepdims=True)
    )
    residual_full = hidden_grad.astype(jnp.bfloat16)
    residual_grad = lax.dynamic_slice_in_dim(residual_full, slot_index * quarter, quarter, 0)[None]
    gain_part = jnp.dot(onehot.T, norm_grad * normed_f, precision=lax.Precision.HIGHEST)
    gain_grad = gain_sum(gain_part, dp, slots)
    block_width = queries.shape[2]
    grad_block = lax.dynamic_slice_in_dim(residual_full, slot_index * block_width, block_width, 1)[
        None
    ]
    query_grad, key_grad, value_grad = causal_backward(
        grad_block, queries, keys, values, attended_block, probs, probs_b
    )
    return (
        output, residual_grad, query_grad, key_grad, value_grad, up_grad[None], down_grad[None], gain_grad,
    )


def flip(index, offset):
    bit = 1
    while bit <= offset:
        if offset & bit:
            index = index + bit - 2 * bit * (lax.div(index, bit) % 2)
        bit *= 2
    return index


def block_mask(rows):
    row = lax.broadcasted_iota(jnp.int32, (rows, rows), 0)
    col = lax.broadcasted_iota(jnp.int32, (rows, rows), 1)
    return (row // LENGTH == col // LENGTH) & (col <= row)


def stack_heads(block):
    heads = block.shape[1] // HD
    return jnp.concatenate([block[:, h * HD : (h + 1) * HD] for h in range(heads)], axis=0)


def attend(query, key, value):
    scores = contract_last(query, key) * HD ** (-0.5)
    scores = jnp.where(block_mask(query.shape[0]), scores, -1e30)
    top = jnp.max(scores, axis=-1, keepdims=True)
    weight = jnp.exp(scores - top)
    probs = weight / jnp.sum(weight, axis=-1, keepdims=True)
    probs_b = probs.astype(jnp.bfloat16)
    attended = jnp.dot(probs_b, value, preferred_element_type=jnp.float32).astype(jnp.bfloat16)
    return attended, probs, probs_b


def layer_kernel(
    dims, labels_ref, modality_ref, query_hbm, key_hbm, value_hbm, residual_hbm, gains_hbm, up_hbm, down_hbm, cot_hbm,
    act_out, pre_grad_out, rows_out, sums_ref, gain_grad_ref, heads_ref,
    gain_ref, up_w, down_w, rows_all, query_s, key_s, value_s, residual_s, gains_s, hidden_s, attended_s, probs_s, probs_b_s, packed,
    stat, tags, pre_t, back_t,
    act_t, pre_grad_t, act_n, pre_grad_n, parts, from_core, from_second, from_first, from_line, gain_mine, gain_inbox,
    gain_own, load_sem, weight_sem, tag_send, tag_recv, stat_send, stat_recv, line_send, line_recv, first_send, first_recv,
    second_send, second_recv, core_send, core_recv, r1_send, r1_recv, r2_send, r2_recv, r3_send, r3_recv,
    r4_send, r4_recv, spread_send, spread_recv, gs_send, gs_recv, gd_send, gd_recv, gx_send, gx_recv, store_sem,
):
    lines, dp, slots, quarter, hidden_units = dims
    width = quarter * slots
    d, s = lax.axis_index("dp"), lax.axis_index("sect")
    line, inner = lax.div(d, 2), d % 2
    y, c = lax.div(s, 2), s % 2
    tokens = dp * LENGTH

    core_id = (d, flip(s, 1))
    turn = [c, 1 - c]
    first_id = [(d + (1 - t) * (1 - 2 * inner), s + t * 2 * (1 - 2 * y)) for t in turn]
    second_id = [first_id[1], first_id[0]]

    def send(src, dst, send_sem, recv_sem, target):
        return remote(src, dst, send_sem, recv_sem, target[0], target[1])

    def line_id(k):
        return (flip(line, k) * 2 + inner, s)

    def side(a, far_first, far_second):
        dy = far_second * (1 - turn[a]) + far_first * turn[a]
        di = far_first * (1 - turn[a]) + far_second * turn[a]
        return y + dy * (1 - 2 * y), inner + di * (1 - 2 * inner), dy * 2 + di

    mine = rows_all.at[0, s, inner, line]
    loads = [
        pltpu.make_async_copy(cot_hbm.at[0, :, pl.ds(pl.multiple_of(s * quarter, quarter), quarter)], mine, load_sem.at[0]),
        pltpu.make_async_copy(query_hbm.at[0], query_s, load_sem.at[1]),
        pltpu.make_async_copy(key_hbm.at[0], key_s, load_sem.at[2]),
        pltpu.make_async_copy(value_hbm.at[0], value_s, load_sem.at[3]),
        pltpu.make_async_copy(
            residual_hbm.at[0, :, pl.ds(pl.multiple_of(s * quarter, quarter), quarter)], residual_s, load_sem.at[4]
        ),
        pltpu.make_async_copy(gains_hbm, gains_s, load_sem.at[5]),
    ]
    for one in loads:
        one.start()
    order = [y * 2, y * 2 + 1, (1 - y) * 2, (1 - y) * 2 + 1]

    def weight_load(which, step):
        src, dst = ((down_hbm, down_w), (up_hbm, up_w))[which]
        at = order[step]
        return pltpu.make_async_copy(
            src.at[0, :, pl.ds(pl.multiple_of(at * quarter, quarter), quarter)], dst.at[at], weight_sem.at[which, step]
        )

    for step in range(slots):
        weight_load(0, step).start()

    lane = lax.broadcasted_iota(jnp.int32, (8, tokens), 1)
    sub = lax.broadcasted_iota(jnp.int32, (LENGTH, HD), 0)
    base = (inner * lines + line) * LENGTH
    tag = jnp.zeros((8, tokens), jnp.float32)
    own_tag = jnp.zeros((LENGTH, HD), jnp.float32)
    for t in range(LENGTH):
        value = labels_ref[0, t].astype(jnp.float32)
        tag = jnp.where(lane == base + t, value, tag)
        own_tag = jnp.where(sub == t, value, own_tag)
    tags[0] = tag

    barrier = pltpu.get_barrier_semaphore()
    for k in range(1, dp):
        pl.semaphore_signal(barrier, inc=1, device_id=(flip(d, k), s), device_id_type=MESH)
    for k in range(1, slots):
        pl.semaphore_signal(barrier, inc=1, device_id=(d, flip(s, k)), device_id_type=MESH)

    def on_line(a, k, where):
        block = rows_all.at[a, s, inner, where]
        return send(block, block, line_send.at[a, k], line_recv.at[a, k], line_id(k))

    def on_first(a, k):
        block = rows_all.at[a, s, inner, flip(line, k)]
        return send(block, block, first_send.at[a, k], first_recv.at[a, k], first_id[a])

    def on_second(a, f, k):
        gy, gi, _ = side(a, f, 0)
        block = rows_all.at[a, gy * 2 + c, gi, flip(line, k)]
        return send(block, block, second_send.at[a, f, k], second_recv.at[a, f, k], second_id[a])

    def on_core(a, f, g):
        gy, gi, place = side(a, f, g)
        group = rows_all.at[a, gy * 2 + c, gi]
        return send(group, group, core_send.at[a, place], core_recv.at[a, place], core_id)

    def gather_start(a):
        for k in range(1, lines):
            on_line(a, k, line).start()
        on_first(a, 0).start()
        on_second(a, 0, 0).start()

    def gather_line(a, k):
        on_line(a, k, line).wait_recv()
        on_first(a, k).start()
        on_second(a, 0, k).start()
        if k == lines - 1:
            on_core(a, 0, 0).start()

    def gather_first(a, k):
        on_first(a, k).wait_recv()
        on_second(a, 1, k).start()
        if k == lines - 1:
            on_core(a, 1, 0).start()

    def gather_second(a, f):
        for k in range(lines):
            on_second(a, f, k).wait_recv()
        on_core(a, f, 1).start()

    def gather_core(a, dy):
        for di in range(2):
            group = rows_all.at[a, 0, 0]
            send(group, group, core_send.at[a, dy * 2 + di], core_recv.at[a, dy * 2 + di], core_id).wait_recv()

    def gather_end(a):
        for k in range(1, lines):
            on_line(a, k, line).wait_send()
        for k in range(lines):
            on_first(a, k).wait_send()
            for f in range(2):
                on_second(a, f, k).wait_send()
        for f in range(2):
            for g in range(2):
                on_core(a, f, g).wait_send()

    def send_tag(k):
        return send(tags.at[0], tags.at[k], tag_send.at[k], tag_recv.at[k], (flip(d, k), s))

    def send_stat(turn, k):
        return send(stat.at[turn, 0], stat.at[turn, k], stat_send.at[turn, k], stat_recv.at[turn, k], (d, flip(s, k)))

    for one in loads:
        one.wait()
    attended, probs, probs_b = attend(stack_heads(query_s[...]), stack_heads(key_s[...]), stack_heads(value_s[...]))
    attended_s[...] = attended
    probs_s[...] = probs
    probs_b_s[...] = probs_b
    square = jnp.zeros((LENGTH, 1), jnp.float32)
    for h in range(quarter // HD):
        cols = slice(h * HD, (h + 1) * HD)
        hid = (
            residual_s[:, cols].astype(jnp.float32) + attended[h * LENGTH : (h + 1) * LENGTH, :].astype(jnp.float32)
        ).astype(jnp.bfloat16)
        hidden_s[:, cols] = hid
        hid_f = hid.astype(jnp.float32)
        square = square + jnp.sum(hid_f * hid_f, axis=-1, keepdims=True)
    stat[0, 0] = jnp.broadcast_to(square, (LENGTH, HD))
    pl.semaphore_wait(barrier, dp - 1 + slots - 1)
    for k in range(1, slots):
        send_stat(0, k).start()
    gather_start(0)
    for k in range(1, dp):
        send_tag(k).start()
    for k in range(1, slots):
        send_stat(0, k).wait_recv()
    total = (stat[0, 0] + stat[0, 1] + stat[0, 2] + stat[0, 3])[:, :1]
    inverse = lax.rsqrt(total / width + 1e-05)

    def gain_rows():
        g = gains_s[:, pl.ds(pl.multiple_of(s * quarter, quarter), quarter)]
        own = own_tag[:, :1]
        return jnp.where(own == 0.0, g[0:1, :], jnp.where(own == 1.0, g[1:2, :], g[2:3, :]))

    rows_all[1, s, inner, line] = (hidden_s[...].astype(jnp.float32) * inverse * gain_rows()).astype(jnp.bfloat16)
    gather_start(1)
    gather_first(0, 0)
    for k in range(1, lines):
        gather_line(0, k)
    gather_first(1, 0)
    weight_load(1, 0).start()
    for k in range(1, lines):
        gather_first(0, k)
        gather_line(1, k)
    weight_load(1, 1).start()

    half = hidden_units // 2

    def project(a, step, parts=(0, 1)):
        dst, weight = ((back_t, down_w), (pre_t, up_w))[a]
        at = order[step]
        if 0 in parts:
            weight_load(a, step).wait()
        block = rows_all[a, at].reshape(tokens, quarter)
        for h in [half * part for part in parts]:
            term = contract_last(weight[at, h : h + half, :], block)
            if step == 0:
                dst[h : h + half, :] = term
            else:
                dst[h : h + half, :] += term

    gather_second(0, 0)
    gather_core(0, 0)
    project(0, 0, (0,))
    gather_first(1, 1)
    project(0, 0, (1,))
    gather_first(1, 2)
    project(0, 1, (0,))
    for k in range(3, lines):
        gather_first(1, k)
    weight_load(1, 2).start()
    weight_load(1, 3).start()
    project(0, 1, (1,))
    gather_second(0, 1)
    gather_core(0, 1)
    project(0, 2)
    gather_second(1, 0)
    project(0, 3)
    gather_core(1, 0)
    project(1, 0)
    gather_second(1, 1)
    project(1, 1)
    gather_core(1, 1)
    project(1, 2)
    project(1, 3)
    keep_rows = pltpu.make_async_copy(rows_all, rows_out, store_sem.at[0])
    keep_rows.start()

    for k in range(1, dp):
        send_tag(k).wait_recv()
    all_tags = tags[0]
    for k in range(1, dp):
        all_tags = all_tags + tags[k]
    modality = modality_ref[s].astype(jnp.float32)
    keep = all_tags[:1, :] == modality
    preact = pre_t[...]
    sigma = jax.nn.sigmoid(preact)
    pre_grad = jnp.where(keep, back_t[...] * sigma * (1.0 + preact * (1.0 - sigma)), 0.0)
    pre_grad_t[...] = pre_grad.astype(jnp.bfloat16)
    pre_grad_n[...] = pre_grad.T.astype(jnp.bfloat16)
    keep_act = pltpu.make_async_copy(act_t, act_out, store_sem.at[1])
    keep_pre_grad = pltpu.make_async_copy(pre_grad_t, pre_grad_out, store_sem.at[2])
    keep_pre_grad.start()

    def to_core(a, dy):
        gy = y + dy * (1 - 2 * y)
        return send(parts.at[a, gy * 2 + 1 - c], from_core.at[a, dy], r1_send.at[a, dy], r1_recv.at[a, dy], core_id)

    def to_second(a, f, k):
        gy, gi, _ = side(a, f, 1)
        block = parts.at[a, gy * 2 + c, gi, flip(line, k)]
        return send(block, from_second.at[a, f, k], r2_send.at[a, f, k], r2_recv.at[a, f, k], second_id[a])

    def to_first(a, k):
        gy, gi, _ = side(a, 1, 0)
        block = parts.at[a, gy * 2 + c, gi, flip(line, k)]
        return send(block, from_first.at[a, k], r3_send.at[a, k], r3_recv.at[a, k], first_id[a])

    def to_line(a, k):
        block = parts.at[a, s, inner, flip(line, k)]
        return send(block, from_line.at[a, k], r4_send.at[a, k], r4_recv.at[a, k], line_id(k))

    def partial_sum(a, at):
        source, weight = ((pre_grad_n, up_w), (act_n, down_w))[a]
        term = jnp.dot(source[...], weight[at], preferred_element_type=jnp.float32)
        parts[a, at] = term.astype(jnp.bfloat16).reshape(parts.shape[2:])
        if a == 0:
            rows = rows_all[1, at].reshape(tokens, quarter).astype(jnp.float32)
            g = gains_s[:, pl.ds(pl.multiple_of(at * quarter, quarter), quarter)]
            own = jnp.where(modality == 0.0, g[0:1, :], jnp.where(modality == 1.0, g[1:2, :], g[2:3, :]))
            total = jnp.sum(term * rows, axis=0, keepdims=True) / own
            chunk = width // dp
            for j in range(quarter // chunk):
                for r in range(8):
                    first = j * chunk + r * HD
                    gain_mine[at * (quarter // chunk) + j, r : r + 1, :] = total[:, first : first + HD]

    def add(dst, src):
        dst[...] = (dst[...].astype(jnp.float32) + src[...].astype(jnp.float32)).astype(jnp.bfloat16)

    ways = list(range(1, lines)) + [0]

    def core_near(a):
        other = (1 - y) * 2
        partial_sum(a, other + 1 - c)
        to_core(a, 1).start()
        partial_sum(a, other + c)

    def core_far(a):
        other = (1 - y) * 2
        partial_sum(a, y * 2 + 1 - c)
        to_core(a, 0).start()
        to_core(a, 1).wait_recv()
        add(parts.at[a, other + c], from_core.at[a, 1])
        for k in ways:
            to_second(a, 1, k).start()
        partial_sum(a, s)
        to_core(a, 0).wait_recv()
        add(parts.at[a, s], from_core.at[a, 0])
        for k in ways:
            to_second(a, 0, k).start()

    def second_sums(a):
        gy, gi, _ = side(a, 1, 0)
        for k in ways:
            to_second(a, 1, k).wait_recv()
            add(parts.at[a, gy * 2 + c, gi, flip(line, k)], from_second.at[a, 1, k])
            to_first(a, k).start()

    def side_sum(a, k):
        to_second(a, 0, k).wait_recv()
        to_first(a, k).wait_recv()
        return (
            parts[a, s, inner, flip(line, k)].astype(jnp.float32)
            + from_second[a, 0, k].astype(jnp.float32)
            + from_first[a, k].astype(jnp.float32)
        )

    def first_sums(a):
        for k in range(1, lines):
            parts[a, s, inner, flip(line, k)] = side_sum(a, k).astype(jnp.bfloat16)
            to_line(a, k).start()

    def line_sums(a):
        total = side_sum(a, 0)
        for k in range(1, lines):
            to_line(a, k).wait_recv()
            total = total + from_line[a, k].astype(jnp.float32)
        return total

    def gain_scatter(k):
        target = flip(d, k)
        return send(gain_mine.at[target], gain_inbox.at[k], gs_send.at[k], gs_recv.at[k], (target, s))

    def gain_spread(k):
        return send(gain_own, gain_ref.at[s, d], gd_send.at[k], gd_recv.at[k], (flip(d, k), s))

    def gain_across(k):
        return send(gain_ref.at[s], gain_ref.at[s], gx_send.at[k], gx_recv.at[k], (d, flip(s, k)))

    own = LENGTH // slots
    part = quarter // slots

    def pack(a, block):
        row = lax.broadcasted_iota(jnp.int32, (slots * LENGTH, LENGTH), 0)
        token = lax.broadcasted_iota(jnp.int32, (slots * LENGTH, LENGTH), 1)
        wanted = (row // LENGTH) * own + row % own
        place = (row % LENGTH) // own
        total = jnp.zeros((slots * LENGTH, part), jnp.float32)
        for j in range(slots):
            pick = ((place == j) & (token == wanted)).astype(jnp.bfloat16)
            total = total + jnp.dot(pick, block[:, j * part : (j + 1) * part], preferred_element_type=jnp.float32)
        packed[a] = total.astype(jnp.bfloat16).reshape(slots, LENGTH, part)
        sums_ref[a, s] = packed[a, s]

    def spread(a, k):
        target = flip(s, k)
        return send(packed.at[a, target], sums_ref.at[a, s], spread_send.at[a, k], spread_recv.at[a, k], (d, target))

    core_near(0)
    core_far(0)
    for k in range(1, dp):
        gain_scatter(k).start()
    preact = pre_t[...]
    activated = jnp.where(keep, preact * jax.nn.sigmoid(preact), 0.0)
    act_t[...] = activated.astype(jnp.bfloat16)
    keep_act.start()
    act_n[...] = activated.T.astype(jnp.bfloat16)
    core_near(1)
    second_sums(0)
    core_far(1)
    first_sums(0)
    second_sums(1)
    gain_total = gain_mine[d]
    for k in range(1, dp):
        gain_scatter(k).wait_recv()
        gain_total = gain_total + gain_inbox[k]
    gain_own[...] = gain_total
    gain_ref[s, d] = gain_total
    for k in range(1, dp):
        gain_spread(k).start()
    norm_grad = line_sums(0)
    hid_f = hidden_s[...].astype(jnp.float32)
    normed_f = hid_f * inverse
    scaled = norm_grad * gain_rows()
    own_stat = jnp.sum(scaled * normed_f, axis=-1, keepdims=True)
    stat[1, 0] = jnp.broadcast_to(own_stat, (LENGTH, HD))
    for k in range(1, slots):
        send_stat(1, k).start()
    first_sums(1)
    for k in range(1, dp):
        gain_spread(k).wait_recv()
    for k in range(1, slots):
        gain_across(k).start()
    for k in range(1, slots):
        send_stat(1, k).wait_recv()
    mean = (stat[1, 0] + stat[1, 1] + stat[1, 2] + stat[1, 3])[:, :1] / width
    cot_f = rows_all[0, s, inner, line].astype(jnp.float32)
    res_grad = (cot_f + inverse * (scaled - normed_f * mean)).astype(jnp.bfloat16)
    pack(0, res_grad)
    for k in range(1, slots):
        spread(0, k).start()
    pack(1, (hidden_s[...].astype(jnp.float32) + line_sums(1)).astype(jnp.bfloat16))
    for k in range(1, slots):
        spread(1, k).start()
    query, key, value = (stack_heads(ref[...]) for ref in (query_s, key_s, value_s))
    grad = stack_heads(res_grad)
    probs = probs_s[...]
    value_grad = contract_first(probs_b_s[...], grad)
    dprob = contract_last(grad, value)
    delta = jnp.sum(grad.astype(jnp.float32) * attended_s[...].astype(jnp.float32), axis=-1, keepdims=True)
    dscore = (probs * (dprob - delta) * HD ** (-0.5)).astype(jnp.bfloat16)
    query_grad = jnp.dot(dscore, key, preferred_element_type=jnp.float32)
    key_grad = contract_first(dscore, query)
    for place, heads in ((0, query_grad), (1, key_grad), (2, value_grad)):
        for h in range(quarter // HD):
            heads_ref[place, :, h * HD : (h + 1) * HD] = heads[h * LENGTH : (h + 1) * LENGTH, :].astype(jnp.bfloat16)
    for k in range(1, slots):
        gain_across(k).wait_recv()
    for m in range(MODALITIES):
        total = jnp.zeros(gain_ref.shape[1:], jnp.float32)
        for slot in range(slots):
            serves = (modality_ref[slot] == m).astype(jnp.float32)
            total = total + serves * gain_ref[slot]
        for j in range(dp):
            for r in range(8):
                first = j * (width // dp) + r * HD
                gain_grad_ref[m : m + 1, first : first + HD] = total[j, r : r + 1, :]
    keep_rows.wait()
    keep_act.wait()
    keep_pre_grad.wait()
    for a in range(2):
        gather_end(a)
        for k in range(1, slots):
            send_stat(a, k).wait_send()
        for f in range(2):
            to_core(a, f).wait_send()
            for k in range(lines):
                to_second(a, f, k).wait_send()
        for k in range(lines):
            to_first(a, k).wait_send()
        for k in range(1, lines):
            to_line(a, k).wait_send()
    for k in range(1, dp):
        send_tag(k).wait_send()
        gain_scatter(k).wait_send()
        gain_spread(k).wait_send()
    for k in range(1, slots):
        gain_across(k).wait_send()
    for a in range(2):
        for k in range(1, slots):
            spread(a, k).wait_recv()
            spread(a, k).wait_send()


LENGTH = 16


def layer(dp, slots, labels, slot_modality, queries, keys, values, residual, gains, up_weight, down_weight, cotangent):
    lines = dp // 2
    quarter = queries.shape[2]
    hidden_units = up_weight.shape[1]
    tokens = dp * LENGTH
    width = quarter * slots
    bf, f32 = jnp.bfloat16, jnp.float32
    any_space = pl.BlockSpec(memory_space=pl.ANY)
    scalar = pl.BlockSpec(memory_space=pltpu.SMEM)
    vm = pl.BlockSpec(memory_space=pltpu.VMEM)
    dma = pltpu.SemaphoreType.DMA
    rows_shape = (2, slots, 2, lines, LENGTH, quarter)
    chunk = width // dp
    return pl.pallas_call(
        functools.partial(layer_kernel, (lines, dp, slots, quarter, hidden_units)),
        out_shape=(
            jax.ShapeDtypeStruct((hidden_units, tokens), bf),
            jax.ShapeDtypeStruct((hidden_units, tokens), bf),
            jax.ShapeDtypeStruct(rows_shape, bf),
            jax.ShapeDtypeStruct((2, slots, LENGTH, quarter // slots), bf),
            jax.ShapeDtypeStruct((MODALITIES, width), f32),
            jax.ShapeDtypeStruct((3, LENGTH, quarter), bf),
        ),
        in_specs=[scalar, scalar] + [any_space] * 8,
        out_specs=(any_space, any_space, any_space, vm, vm, vm),
        scratch_shapes=[
            pltpu.VMEM((slots, dp, 8, chunk // 8), f32),
            pltpu.VMEM((slots, hidden_units, quarter), bf),
            pltpu.VMEM((slots, hidden_units, quarter), bf),
            pltpu.VMEM(rows_shape, bf),
            pltpu.VMEM((LENGTH, quarter), bf),
            pltpu.VMEM((LENGTH, quarter), bf),
            pltpu.VMEM((LENGTH, quarter), bf),
            pltpu.VMEM((LENGTH, quarter), bf),
            pltpu.VMEM(gains.shape, f32),
            pltpu.VMEM((LENGTH, quarter), bf),
            pltpu.VMEM((quarter // HD * LENGTH, HD), bf),
            pltpu.VMEM((quarter // HD * LENGTH, quarter // HD * LENGTH), f32),
            pltpu.VMEM((quarter // HD * LENGTH, quarter // HD * LENGTH), bf),
            pltpu.VMEM((2, slots, LENGTH, quarter // slots), bf),
            pltpu.VMEM((2, slots, LENGTH, HD), f32),
            pltpu.VMEM((dp, 8, tokens), f32),
            pltpu.VMEM((hidden_units, tokens), f32),
            pltpu.VMEM((hidden_units, tokens), f32),
            pltpu.VMEM((hidden_units, tokens), bf),
            pltpu.VMEM((hidden_units, tokens), bf),
            pltpu.VMEM((tokens, hidden_units), bf),
            pltpu.VMEM((tokens, hidden_units), bf),
            pltpu.VMEM(rows_shape, bf),
            pltpu.VMEM((2, 2, 2, lines, LENGTH, quarter), bf),
            pltpu.VMEM((2, 2, lines, LENGTH, quarter), bf),
            pltpu.VMEM((2, lines, LENGTH, quarter), bf),
            pltpu.VMEM((2, lines, LENGTH, quarter), bf),
            pltpu.VMEM((dp, 8, chunk // 8), f32),
            pltpu.VMEM((dp, 8, chunk // 8), f32),
            pltpu.VMEM((8, chunk // 8), f32),
            dma((6,)), dma((2, slots)),
            dma((dp,)), dma((dp,)),
            dma((2, slots)), dma((2, slots)),
            dma((2, lines)), dma((2, lines)),
            dma((2, lines)), dma((2, lines)),
            dma((2, 2, lines)), dma((2, 2, lines)),
            dma((2, 4)), dma((2, 4)),
            dma((2, 2)), dma((2, 2)),
            dma((2, 2, lines)), dma((2, 2, lines)),
            dma((2, lines)), dma((2, lines)),
            dma((2, lines)), dma((2, lines)),
            dma((2, slots)), dma((2, slots)),
            dma((dp,)), dma((dp,)),
            dma((dp,)), dma((dp,)),
            dma((slots,)), dma((slots,)),
            dma((3,)),
        ],
        compiler_params=pltpu.CompilerParams(
            collective_id=0, has_side_effects=True, vmem_limit_bytes=62 * 1024 * 1024
        ),
    )(labels, slot_modality, queries, keys, values, residual, gains, up_weight, down_weight, cotangent)


def grads_kernel(
    act_ref, pre_grad_ref, rows_ref, cots_ref, sums_ref, gain_ref, heads_ref,
    out_ref, res_grad_ref, query_grad_ref, key_grad_ref, value_grad_ref, up_grad_ref, down_grad_ref, gain_grad_ref,
):
    step = pl.program_id(0)
    rows = rows_ref[0, 0].reshape(-1, rows_ref.shape[-1])
    cots = cots_ref[0, 0].reshape(-1, cots_ref.shape[-1])
    up_grad_ref[...] = jnp.dot(pre_grad_ref[...], rows, preferred_element_type=jnp.float32).astype(jnp.bfloat16)
    down_grad_ref[...] = jnp.dot(act_ref[...], cots, preferred_element_type=jnp.float32).astype(jnp.bfloat16)

    @pl.when(step == 1)
    def _():
        for place, ref in enumerate((query_grad_ref, key_grad_ref, value_grad_ref)):
            ref[0] = heads_ref[place]
        gain_grad_ref[...] = gain_ref[...]
        slots, part = sums_ref.shape[1], sums_ref.shape[3]
        own = LENGTH // slots
        for a, ref in ((0, res_grad_ref), (1, out_ref)):
            for q in range(slots):
                packed = sums_ref[a, q].astype(jnp.float32)
                for j in range(slots):
                    first = (q * slots + j) * part
                    ref[0, :, first : first + part] = packed[j * own : (j + 1) * own, :].astype(jnp.bfloat16)


def grads(act, pre_grad, rows, sums, gain, heads, width):
    hidden_units, tokens = act.shape
    _, slots, inner, lines, length, quarter = rows.shape
    bf, f32 = jnp.bfloat16, jnp.float32
    halves = 2
    columns = quarter // halves

    def whole(shape):
        return pl.BlockSpec(shape, lambda i: (0,) * len(shape))

    def block(a):
        return pl.BlockSpec(
            (1, 1, inner, lines, length, columns), lambda i: (a, i // halves, 0, 0, 0, i % halves)
        )

    own = (1, length // slots, width)
    head = (1, length, quarter)
    weight = pl.BlockSpec((hidden_units, columns), lambda i: (0, i))
    return pl.pallas_call(
        grads_kernel,
        grid=(slots * halves,),
        out_shape=(
            jax.ShapeDtypeStruct(own, bf),
            jax.ShapeDtypeStruct(own, bf),
            jax.ShapeDtypeStruct(head, bf),
            jax.ShapeDtypeStruct(head, bf),
            jax.ShapeDtypeStruct(head, bf),
            jax.ShapeDtypeStruct((hidden_units, width), bf),
            jax.ShapeDtypeStruct((hidden_units, width), bf),
            jax.ShapeDtypeStruct((MODALITIES, width), f32),
        ),
        in_specs=[
            whole(act.shape), whole(act.shape), block(1), block(0), whole(sums.shape), whole(gain.shape),
            whole(heads.shape),
        ],
        out_specs=(
            whole(own), whole(own), whole(head), whole(head), whole(head), weight, weight, whole((MODALITIES, width)),
        ),
        compiler_params=pltpu.CompilerParams(
            dimension_semantics=("arbitrary",), vmem_limit_bytes=VMEM_BYTES
        ),
    )(act, pre_grad, rows, rows, sums, gain, heads)


def fast_on_device(
    dp, slots, queries, keys, values, residual, labels, slot_modality, gains, up_weight, down_weight, cotangent
):
    act, pre_grad, rows, sums, gain, heads = layer(
        dp, slots, labels, slot_modality, queries, keys, values, residual, gains, up_weight, down_weight, cotangent
    )
    output, residual_grad, query_grad, key_grad, value_grad, up_grad, down_grad, gain_grad = grads(
        act, pre_grad, rows, sums, gain, heads, residual.shape[2]
    )
    return (
        output, residual_grad, query_grad, key_grad, value_grad, up_grad[None], down_grad[None], gain_grad,
    )


def solution(mesh):
    in_specs = (
        P("dp", None, "sect"),
        P("dp", None, "sect"),
        P("dp", None, "sect"),
        P("dp", None, None),
        P("dp", None),
        P(),
        P(),
        P("sect", "dp", None),
        P("sect", "dp", None),
        P("dp", None, None),
    )
    out_specs = (
        P("dp", "sect", None),
        P("dp", "sect", None),
        P("dp", None, "sect"),
        P("dp", None, "sect"),
        P("dp", None, "sect"),
        P("sect", "dp", None),
        P("sect", "dp", None),
        P(),
    )
    dp, slots = mesh.shape["dp"], mesh.shape["sect"]
    body = functools.partial(fast_on_device if (dp, slots) == (8, 4) else on_device, dp, slots)
    return jax.shard_map(
        body, mesh=mesh, in_specs=in_specs, out_specs=out_specs, check_vma=False
    )
```
